256 devices in a mesh: seq: 64 (over x, z_hi, y), rep: 4 (over z_lo, core).
Axes of the slice: x: 4, y: 4, z: 8 (z_hi: 4, z_lo: 2; z = z_hi * 2 + z_lo), core: 2. Of those that a mesh axis runs over, the one named last changes fastest.
Arguments:
- tokens: bfloat16 [8192, 2048], P('seq'), may hold values from -6 to 6
- prior_cache: bfloat16 [2048, 576], P('seq'), may hold values from -6 to 6
- attn_gain: float32 [2048], replicated, may hold values from 0.25 to 1.75
- q_weight: bfloat16 [2048, 1536], P(None, 'rep'), may hold values from -0.125 to 0.125
- kv_weight: bfloat16 [2048, 576], replicated, may hold values from -0.125 to 0.125
- kv_gain: float32 [512], replicated, may hold values from 0.25 to 1.75
- key_up: bfloat16 [8, 128, 512], P('rep'), may hold values from -18.561553006146873 to 18.561553006146873
- value_up: bfloat16 [8, 512, 128], P('rep'), may hold values from -0.25 to 0.25
- out_weight: bfloat16 [1024, 2048], P('rep'), may hold values from -0.1875 to 0.1875
- moe_gain: float32 [2048], replicated, may hold values from 0.25 to 1.75
- router: bfloat16 [2048, 64], replicated, may hold values from -0.125 to 0.125
- expert_ids: int32 [8192, 6], P('seq'), may hold values from 0 to 63, all different within a row; in each aligned block of 32 rows (0 to 31, 32 to 63, ...) at most 4 rows name the same one
- w_gate: bfloat16 [64, 2048, 1408], P('seq', None, 'rep'), may hold values from -0.125 to 0.125
- w_up: bfloat16 [64, 2048, 1408], P('seq', None, 'rep'), may hold values from -0.125 to 0.125
- w_down: bfloat16 [64, 1408, 2048], P('seq', 'rep'), may hold values from -0.15625 to 0.15625
- handover: bfloat16 [256, 1, 1024, 576], P('rep', None, 'seq'), may hold values from -6 to 6
- lengths: int32 [256], replicated, may hold values from 1 to 1024, 65536 in all
- request_owner: int32 [256], replicated, may hold values from 0 to 63, as said below
- page_table: int32 [256, 8], replicated, may hold values from 0 to 7, as said below
Outputs:
- layer_out: bfloat16 [8192, 2048], P(('seq', 'rep'))
- decode_pages: bfloat16 [2048, 1, 128, 576], P(('seq', 'rep'))
The draws below stay inside these ranges and needn't reach their ends.
Inputs may be any that keep to these rules, and one draw needn't show every extreme that they name: `request_owner`: the requests form 4 consecutive groups of 256 / 4; within each group every value is taken by exactly 1 request. `page_table`: for the requests of one group with the same owner, the entries of their rows together are each of 0 to 7 once. `expert_ids`: each row names 6 different experts; in each aligned block of 32 rows no expert is named by more than 4 rows, a bound that some block reaches. The lengths sum to 65536; the largest is 1024.
All inputs are finite; a program needn't handle non-finite values.
Results may differ from the reference program's by a relative error of at most 0.035.
Values may be sent and summed in bfloat16 or wider, within the bound.
A program may use at most 128 MiB of HBM per device.

```python
import math
import jax
import jax.numpy as jnp
import numpy as np
from jax import lax

D = 2048
HEADS = 8
NOPE = 128
ROPE = 64
VDIM = 128
LAT = 512
LATC = 576
FFE = 1408
TOP = 6
EXPERTS = 64
TOKENS = 8192
PRIOR = 2048
QTOK = 32
SQ = 4
HL = 1
REQ_DEV = 1
PAGE = 128
MAXLEN = 1024
PPR = 8
REQS = 256
HANDED = 65536
N_SEQ = 64
N_REP = 4


def assignment(key):
    group_size = N_SEQ * REQ_DEV
    pool_size = REQ_DEV * PPR
    group_keys = jax.random.split(jax.random.fold_in(key, 7), N_REP)
    orders = jax.vmap(lambda subkey: jax.random.permutation(subkey, group_size))(group_keys)
    owners = (orders // REQ_DEV).reshape(-1).astype(jnp.int32)
    slot_rank = (orders % REQ_DEV).reshape(-1).astype(jnp.int32)
    pool_keys = jax.random.split(jax.random.fold_in(key, 11), N_SEQ * N_REP)
    shuffles = jax.vmap(lambda subkey: jax.random.permutation(subkey, pool_size))(pool_keys)
    device_of = owners * N_REP + (jnp.arange(REQS) // group_size).astype(jnp.int32)
    places = slot_rank[:, None] * PPR + jnp.arange(PPR).astype(jnp.int32)[None, :]
    tables = shuffles[device_of[:, None], places]
    return (owners, tables.astype(jnp.int32))


def draw_request_owner(key, part):
    return assignment(key)[0]


def draw_page_table(key, part):
    return assignment(key)[1]


def draw_key_up(key, part):
    head_ranks = jax.random.permutation(jax.random.fold_in(key, 3), HEADS).astype(jnp.float32)
    strength = 100.0 ** (head_ranks / (HEADS - 1))
    entry_key = jax.random.fold_in(key, 5)
    entries = jnp.clip(jax.random.normal(entry_key, (HEADS, NOPE, LAT), jnp.float32), -4.0, 4.0)
    return (entries * strength[:, None, None] * LAT ** (-0.5)).astype(jnp.bfloat16)


def block_scale(own_key, shape, cuts, smallest, largest):
    level = 1.0
    for dim, blocks in cuts:
        steps = jax.random.uniform(jax.random.fold_in(jax.random.fold_in(own_key, 6), dim), (blocks,), jnp.float32, smallest / len(cuts), largest / len(cuts))
        level = level * jnp.repeat(jnp.exp(steps), shape[dim] // blocks).reshape((-1,) + (1,) * (len(shape) - 1 - dim))
    return level


def length_profile(number_of, total, limit, skew):
    loads = [(1 << 20) // math.isqrt(grade ** skew) + 1 for grade in range(2, number_of + 1)]
    surplus, holding = total - limit - (number_of - 1), [1] * (number_of - 1)
    while surplus > 0:
        candidates = [i for i in range(number_of - 1) if holding[i] < limit]
        whole, left = sum([loads[i] for i in candidates]), surplus
        for i in candidates:
            more = min(limit - holding[i], max(1, left * loads[i] // whole), surplus)
            holding[i] = holding[i] + more
            surplus = surplus - more
    return np.array([limit] + holding)


def uneven_parts(key, amount, total, bound, skew):
    if amount == 2:
        one = jax.random.randint(key, (), max(1, total - bound), min(bound, total - 1) + 1)
        return jnp.stack([one, total - one])
    tallies = jnp.asarray(length_profile(amount, total, bound, skew), jnp.int32)
    pairs = (amount - 1) // 2
    donor, sink = tallies[1:1 + 2 * pairs:2], tallies[2:2 + 2 * pairs:2]
    room = jnp.minimum(donor - 1, bound - sink)
    moved = jax.random.randint(jax.random.fold_in(key, 1), (pairs,), 0, 1 << 20) % (room + 1)
    tallies = tallies.at[1:1 + 2 * pairs:2].set(donor - moved).at[2:2 + 2 * pairs:2].set(sink + moved)
    return tallies[jax.random.permutation(jax.random.fold_in(key, 2), amount)]


def deal_out(key, own, number, rows, number_of, top, reach, lean):
    ranking = jax.random.permutation(key, number_of)
    packed, ordinary = portions_of(number_of, rows * top, reach, lean, True), portions_of(number_of, rows * top, reach, lean, False)
    places = jnp.arange(number_of)

    def named(tallies, turn):
        used = int((tallies > 0).sum())
        fixed = max(1, used // 4)
        passed = fixed + (places - fixed + turn * (used - fixed)) % max(1, number_of - fixed)
        return jnp.zeros((number_of,), jnp.int32).at[ranking[jnp.where(places < fixed, places, passed)]].set(jnp.asarray(tallies, jnp.int32))

    tallies = jnp.where(number % 4 == 0, named(packed, number // 4), named(ordinary, number - number // 4 - 1))
    mixed = jax.random.permutation(jax.random.fold_in(own, 3), number_of)
    source_of, receiver = mixed[0:number_of // 2 * 2:2], mixed[1:number_of // 2 * 2:2]
    room = jnp.minimum(tallies[source_of] - 1, reach - tallies[receiver]) // 2
    room = jnp.where((source_of == ranking[0]) | (receiver == ranking[0]) | (tallies[receiver] == 0), 0, jnp.maximum(room, 0))
    passed = jax.random.randint(jax.random.fold_in(own, 4), (number_of // 2,), 0, 1 << 20) % (room + 1)
    tallies = tallies.at[source_of].add(-passed).at[receiver].add(passed)
    labels = jnp.searchsorted(jnp.cumsum(tallies), jnp.arange(rows * top), side="right").astype(jnp.int32)
    grid = labels.reshape(top, rows).T
    grid = grid[jax.random.permutation(jax.random.fold_in(own, 1), rows)]
    turn = jax.random.randint(jax.random.fold_in(own, 2), (rows, 1), 0, top)
    return jnp.take_along_axis(grid, (jnp.arange(top)[None, :] + turn) % top, axis=1)


def portions_of(count, total, most, slope, full):
    loads = [(1 << 20) // math.isqrt(standing ** slope) + 1 for standing in range(1, count + 1)]
    largest = most if full else min(most, max(-(-total // count), total * loads[0] // sum(loads)))
    least = 1 if total - largest >= count - 1 else 0
    counts, surplus = [largest] + [least] * (count - 1), total - largest - least * (count - 1)
    while surplus > 0:
        free = [i for i in range(1, count) if counts[i] < largest] or [i for i in range(1, count) if counts[i] < most]
        pool, remaining = sum([loads[i] for i in free]), surplus
        for i in free:
            more = min(most - counts[i], max(1, remaining * loads[i] // pool), surplus)
            counts[i] = counts[i] + more
            surplus = surplus - more
    return np.array(counts)


def scatter_about(key, extent, scale, limit, pieces=(), kind=jnp.bfloat16):
    values = scale * jax.random.normal(key, extent, jnp.float32)
    if pieces:
        values = values * block_scale(key, extent, pieces, -0.22, 0.18)
    return jnp.clip(values, -limit, limit).astype(kind)


def setup_inputs(seed: int = 0) -> dict:
    keys = jax.random.split(jax.random.key(seed), 20)
    tokens = scatter_about(keys[0], (TOKENS, D), 1.0, 6.0, ((0, 64),))
    prior_cache = scatter_about(keys[1], (PRIOR, LATC), 1.0, 6.0, ((0, 64),))
    attn_gain = jnp.clip(1.0 + 0.15 * jax.random.normal(keys[2], (D,), jnp.float32), 0.25, 1.75)
    q_weight = scatter_about(keys[3], (D, HEADS * (NOPE + ROPE)), D ** -0.5, 0.125, ((1, 4),))
    kv_weight = scatter_about(keys[4], (D, LATC), D ** -0.5, 0.125)
    kv_gain = jnp.clip(1.0 + 0.15 * jax.random.normal(keys[5], (LAT,), jnp.float32), 0.25, 1.75)
    key_up = draw_key_up(jax.random.fold_in(keys[19], 71), 0)
    value_up = scatter_about(keys[7], (HEADS, LAT, VDIM), LAT ** -0.5, 0.25, ((0, 4),))
    out_weight = scatter_about(keys[8], (HEADS * VDIM, D), (HEADS * VDIM) ** -0.5, 0.1875, ((0, 4),))
    moe_gain = jnp.clip(1.0 + 0.15 * jax.random.normal(keys[9], (D,), jnp.float32), 0.25, 1.75)
    router = scatter_about(keys[10], (D, EXPERTS), D ** -0.5, 0.125)
    expert_ids_keys = jax.random.split(jax.random.fold_in(keys[11], 1), TOKENS // QTOK)
    expert_ids_turns = jax.random.permutation(jax.random.fold_in(keys[11], 3), TOKENS // QTOK)
    expert_ids = jax.vmap(lambda own, number: deal_out(jax.random.fold_in(keys[11], 2), own, number, QTOK, EXPERTS, TOP, SQ, 1))(expert_ids_keys, expert_ids_turns).reshape((TOKENS, TOP))
    w_gate = scatter_about(keys[12], (EXPERTS, D, FFE), D ** -0.5, 0.125, ((0, 64), (2, 4)))
    w_up = scatter_about(keys[13], (EXPERTS, D, FFE), D ** -0.5, 0.125, ((0, 64), (2, 4)))
    w_down = scatter_about(keys[14], (EXPERTS, FFE, D), FFE ** -0.5, 0.15625, ((0, 64), (1, 4)))
    handover = scatter_about(keys[15], (REQS, HL, MAXLEN, LATC), 1.0, 6.0, ((0, 4), (2, 64)))
    lengths = uneven_parts(keys[16], REQS, HANDED, MAXLEN, 2).astype(jnp.int32)
    request_owner = draw_request_owner(jax.random.fold_in(keys[19], 71), 0)
    page_table = draw_page_table(jax.random.fold_in(keys[19], 71), 0)
    return {"tokens": tokens, "prior_cache": prior_cache, "attn_gain": attn_gain, "q_weight": q_weight, "kv_weight": kv_weight, "kv_gain": kv_gain, "key_up": key_up, "value_up": value_up, "out_weight": out_weight, "moe_gain": moe_gain, "router": router, "expert_ids": expert_ids, "w_gate": w_gate, "w_up": w_up, "w_down": w_down, "handover": handover, "lengths": lengths, "request_owner": request_owner, "page_table": page_table}


epsilon = 1e-06
rope_base = 50000.0
route_scale = 2.446

def rms_scale(values, gain_vector):
    return values * lax.rsqrt(lax.optimization_barrier(jnp.mean(values * values, axis=-1, keepdims=True)) + epsilon) * gain_vector

def rotate(values, positions):
    half_width = values.shape[-1] // 2
    frequency = rope_base ** (-jnp.arange(half_width).astype(jnp.float32) / half_width)
    angles = positions.astype(jnp.float32).reshape((-1,) + (1,) * (values.ndim - 2) + (1,)) * frequency
    cosine = jnp.cos(angles)
    sine_values = jnp.sin(angles)
    front_half = values[..., :half_width]
    back_half = values[..., half_width:]
    return jnp.concatenate([front_half * cosine - back_half * sine_values, back_half * cosine + front_half * sine_values], axis=-1)

def reference(tokens, prior_cache, attn_gain, q_weight, kv_weight, kv_gain, key_up, value_up, out_weight, moe_gain, router, expert_ids, w_gate, w_up, w_down, handover, lengths, request_owner, page_table):
    token_float = tokens.astype(jnp.float32)
    normed = rms_scale(token_float, attn_gain).astype(jnp.bfloat16)
    positions = PRIOR + jnp.arange(TOKENS).astype(jnp.int32)
    projected = jnp.dot(normed, q_weight, preferred_element_type=jnp.float32).reshape(TOKENS, HEADS, NOPE + ROPE)
    q_nope = projected[..., :NOPE].astype(jnp.bfloat16)
    q_rope = rotate(projected[..., NOPE:], positions)
    latent = jnp.dot(normed, kv_weight, preferred_element_type=jnp.float32)
    span_keys = jnp.concatenate([rms_scale(latent[:, :LAT], kv_gain), rotate(latent[:, LAT:], positions)], axis=1).astype(jnp.bfloat16)
    all_keys = jnp.concatenate([prior_cache, span_keys], axis=0)
    q_latent = jnp.einsum('thn,hnc->thc', q_nope.astype(jnp.float32), key_up.astype(jnp.float32))
    queries = jnp.concatenate([q_latent, q_rope], axis=2).astype(jnp.bfloat16)
    key_pos = (jnp.arange(PRIOR + TOKENS) - PRIOR).astype(jnp.int32)
    key_pos = jnp.where(key_pos < 0, -1, key_pos).astype(jnp.int32)
    score_scale = (NOPE + ROPE) ** (-0.5)
    query_block = min(512, TOKENS)

    def attend(head):
        head_rows = jnp.take(queries, head, axis=1)

        def one_block(first_row):
            row_block = lax.dynamic_slice_in_dim(head_rows, first_row, query_block, 0)
            scores = lax.dot_general(row_block, all_keys, (((1,), (1,)), ((), ())), preferred_element_type=jnp.float32) * score_scale
            query_pos = (first_row + jnp.arange(query_block)).astype(jnp.int32)
            scores = jnp.where(key_pos[None, :] <= query_pos[:, None], scores, -1e+30)
            row_max = lax.optimization_barrier(jnp.max(scores, axis=1, keepdims=True))
            weight = jnp.exp(scores - row_max)
            row_sum = lax.optimization_barrier(jnp.sum(weight, axis=1, keepdims=True))
            summed = jnp.dot(weight.astype(jnp.bfloat16), all_keys[:, :LAT], preferred_element_type=jnp.float32)
            return (summed / row_sum).astype(jnp.bfloat16)
        starts = jnp.arange(0, TOKENS, query_block).astype(jnp.int32)
        return lax.map(one_block, starts).reshape(TOKENS, LAT)
    head_latent = lax.map(attend, jnp.arange(HEADS).astype(jnp.int32))
    heads_out = jnp.einsum('htc,hcv->thv', head_latent.astype(jnp.float32), value_up.astype(jnp.float32)).astype(jnp.bfloat16).reshape(TOKENS, HEADS * VDIM)
    hidden_state = token_float + jnp.dot(heads_out, out_weight, preferred_element_type=jnp.float32)
    moe_in = rms_scale(hidden_state, moe_gain).astype(jnp.bfloat16)
    logits = jnp.dot(moe_in, router, preferred_element_type=jnp.float32)
    chosen = jnp.take_along_axis(logits, expert_ids, axis=1)
    gate_score = jax.nn.sigmoid(chosen)
    weights = route_scale * gate_score / lax.optimization_barrier(jnp.sum(gate_score, axis=1, keepdims=True))
    flat_ids = expert_ids.reshape(-1)
    flat_weights = weights.reshape(-1)
    row_total = TOKENS * TOP
    room = TOKENS // QTOK * SQ

    def expert_step(running, expert):
        picked = jnp.nonzero(flat_ids == expert, size=room, fill_value=row_total)[0].astype(jnp.int32)
        live_mask = picked < row_total
        clipped = jnp.minimum(picked, row_total - 1)
        token_rows = clipped // TOP
        expert_rows = jnp.take(moe_in, token_rows, axis=0)
        gate_sum = jnp.dot(expert_rows, w_gate[expert], preferred_element_type=jnp.float32)
        up_sum = jnp.dot(expert_rows, w_up[expert], preferred_element_type=jnp.float32)
        activated = (jax.nn.silu(gate_sum) * up_sum).astype(jnp.bfloat16)
        expert_out = jnp.dot(activated, w_down[expert], preferred_element_type=jnp.float32).astype(jnp.bfloat16)
        added = jnp.where(live_mask[:, None], flat_weights[clipped][:, None] * expert_out.astype(jnp.float32), 0.0)
        return (running.at[token_rows].add(added), None)
    moe_sum, _ = lax.scan(expert_step, jnp.zeros((TOKENS, D), jnp.float32), jnp.arange(EXPERTS).astype(jnp.int32))
    layer_out = (hidden_state + moe_sum).astype(jnp.bfloat16)
    group_size = REQS // N_REP
    device_of = request_owner * N_REP + (jnp.arange(REQS) // group_size).astype(jnp.int32)
    physical = (device_of[:, None] * (REQ_DEV * PPR) + page_table).reshape(-1)
    alive_mask = jnp.arange(MAXLEN).astype(jnp.int32)[None, :] < lengths[:, None]
    masked = jnp.where(alive_mask[:, None, :, None], handover, jnp.zeros((), handover.dtype))
    page_rows = masked.reshape(REQS, HL, PPR, PAGE, LATC).transpose(0, 2, 1, 3, 4).reshape(REQS * PPR, HL, PAGE, LATC)
    decode_pages = jnp.zeros((REQS * PPR, HL, PAGE, LATC), handover.dtype).at[physical].set(page_rows)
    return (layer_out, decode_pages)
```

```python
import functools
import jax
import jax.numpy as jnp
from jax import lax
from jax.experimental import pallas as pl
from jax.experimental.pallas import tpu as pltpu
from jax.sharding import PartitionSpec as P

PAGE = 128


epsilon = 1e-06
rope_base = 50000.0
route_scale = 2.446


def cut_along(value, dim, peers):
    lengths = value.shape
    pieces = value.reshape(*lengths[:dim], peers, lengths[dim] // peers, *lengths[dim + 1 :])
    return jnp.moveaxis(pieces, dim, 0)


def sent_and_summed(value, axis, dim):
    pieces = cut_along(value, dim, lax.axis_size(axis))
    arrived = lax.all_to_all(pieces, axis, split_axis=0, concat_axis=0, tiled=True)
    return arrived.astype(jnp.float32).sum(axis=0)


def rms_scale(values, gain_vector):
    return (
        values
        * lax.rsqrt(jnp.mean(values * values, axis=-1, keepdims=True) + epsilon)
        * gain_vector
    )


def rotate(values, positions):
    half_width = values.shape[-1] // 2
    frequency = rope_base ** (-jnp.arange(half_width).astype(jnp.float32) / half_width)
    angles = (
        positions.astype(jnp.float32).reshape((-1,) + (1,) * (values.ndim - 2) + (1,)) * frequency
    )
    cosine = jnp.cos(angles)
    sine_values = jnp.sin(angles)
    front_half = values[..., :half_width]
    back_half = values[..., half_width:]
    return jnp.concatenate(
        [
            front_half * cosine - back_half * sine_values,
            back_half * cosine + front_half * sine_values,
        ],
        axis=-1,
    )


def latent_keys(row_block, positions, kv_weight, kv_gain, latent_width):
    latent = jnp.dot(row_block, kv_weight, preferred_element_type=jnp.float32)
    return jnp.concatenate(
        [rms_scale(latent[:, :latent_width], kv_gain), rotate(latent[:, latent_width:], positions)],
        axis=1,
    ).astype(jnp.bfloat16)


def slot_table(route_ids, experts_total, capacity):
    blocks_here = route_ids.shape[0]
    flat_ids = route_ids.reshape(blocks_here, -1)
    onehot = (flat_ids[:, :, None] == jnp.arange(experts_total)[None, None, :]).astype(jnp.int32)
    row_ranks = jnp.sum((jnp.cumsum(onehot, axis=1) - 1) * onehot, axis=2)
    return flat_ids * capacity + row_ranks


def source_rows(target, slot_count):
    matches = (target[:, None, :] == jnp.arange(slot_count)[None, :, None]).astype(jnp.int32)
    return (jnp.argmax(matches, axis=2), jnp.max(matches, axis=2))


MESH = pl.DeviceIdType.MESH
HALF = 80
LATW = 512
KEYW = 640


def remote(src, dst, send_sem, recv_sem, seq, rep):
    return pltpu.make_async_remote_copy(
        src_ref=src,
        dst_ref=dst,
        send_sem=send_sem,
        recv_sem=recv_sem,
        device_id=(seq, rep),
        device_id_type=MESH,
    )


def greet(partners):
    barrier = pltpu.get_barrier_semaphore()
    for seq, rep in partners:
        pl.semaphore_signal(barrier, inc=1, device_id=(seq, rep), device_id_type=MESH)
    pl.semaphore_wait(barrier, len(partners))


def ring_offset(j):
    return j + jnp.where(j >= 2, 1, 0) - jnp.where(j >= 3, 2, 0)


def attend_kernel(
    scale,
    prior_rows,
    span_rows,
    q_ref,
    own_ref,
    out_ref,
    ring,
    sib,
    acc,
    mx,
    sm,
    local_sem,
    z_send,
    z_recv,
    a_send,
    a_recv,
    a2_send,
    a2_recv,
    b_send,
    b_recv,
    b2_send,
    b2_recv,
    s_send,
    s_recv,
):
    seq = lax.axis_index("seq")
    rep = lax.axis_index("rep")
    core = lax.rem(rep, 2)
    zl = rep // 2
    x0 = seq // 16
    g = lax.rem(seq // 4, 4)
    y0 = lax.rem(seq, 4)
    a0 = x0 + core * (y0 - x0)
    b0 = y0 + core * (x0 - y0)
    sa = 16 - 15 * core
    sb = 1 + 15 * core
    d = 2 * zl - 1
    mate = rep + 1 - 2 * core
    other = rep + 2 - 4 * zl

    def m4(v):
        return lax.rem(v + 4, 4)

    def seq_of(a, z, b):
        return a * sa + z * 4 + b * sb

    a_next = seq_of(m4(a0 + 1), g, b0)
    a_prev = seq_of(m4(a0 - 1), g, b0)
    b_next = seq_of(a0, g, m4(b0 + 1))
    b_prev = seq_of(a0, g, m4(b0 - 1))
    z_to = [
        (seq_of(a0, m4(g + d), b0), other),
        (seq_of(a0, m4(g + d), b0), rep),
        (seq_of(a0, m4(g + 2), b0), other),
    ]
    z_in = [m4(g + d), m4(g - d), m4(g + 2)]
    partners = [
        (a_next, rep),
        (a_prev, rep),
        (b_next, rep),
        (b_prev, rep),
        (seq, mate),
        z_to[0],
        z_to[1],
        (seq_of(a0, m4(g - d), b0), rep),
        z_to[2],
    ]
    zs = [g] + z_in

    def place(j):
        return ring_offset(j)

    own_slot = ring.at[b0, a0, g]
    local = pltpu.make_async_copy(
        own_ref.at[pl.ds(pl.multiple_of(core * HALF, HALF), HALF)], own_slot, local_sem.at[0]
    )
    local_sib = pltpu.make_async_copy(
        own_ref.at[pl.ds(pl.multiple_of((1 - core) * HALF, HALF), HALF)],
        sib.at[a0, b0, g],
        local_sem.at[1],
    )
    local.start()
    local_sib.start()
    mx[...] = jnp.full(mx.shape, -1e30, jnp.float32)
    sm[...] = jnp.zeros(sm.shape, jnp.float32)
    acc[...] = jnp.zeros(acc.shape, jnp.float32)
    local.wait()
    local_sib.wait()
    greet(partners)

    def z_copy(k):
        return remote(own_slot, own_slot, z_send.at[k], z_recv.at[k], z_to[k][0], z_to[k][1])

    def z_arrival(k):
        slot = ring.at[b0, a0, z_in[k]]
        return remote(slot, slot, z_send.at[k], z_recv.at[k], z_to[k][0], z_to[k][1])

    def a_copy(i, k):
        slot = ring.at[b0, a0, zs[k]]
        return remote(slot, slot, a_send.at[i, k], a_recv.at[i, k], (a_next, a_prev)[i], rep)

    def a_arrival(i, k):
        slot = ring.at[b0, m4(a0 + (-1, 1)[i]), zs[k]]
        return remote(slot, slot, a_send.at[i, k], a_recv.at[i, k], (a_next, a_prev)[i], rep)

    def a2_copy(k):
        i = k % 2
        slot = ring.at[b0, m4(a0 + (-1, 1)[i]), zs[k]]
        return remote(slot, slot, a2_send.at[k], a2_recv.at[k], (a_next, a_prev)[i], rep)

    def a2_arrival(k):
        slot = ring.at[b0, m4(a0 + 2), zs[k]]
        return remote(slot, slot, a2_send.at[k], a2_recv.at[k], (a_next, a_prev)[k % 2], rep)

    def b_copy(i, j, k):
        slot = ring.at[b0, m4(a0 + place(j)), zs[k]]
        n = j * 4 + k
        return remote(slot, slot, b_send.at[i, n], b_recv.at[i, n], (b_next, b_prev)[i], rep)

    def b_arrival(i, j, k):
        slot = ring.at[m4(b0 + (-1, 1)[i]), m4(a0 + place(j)), zs[k]]
        n = j * 4 + k
        return remote(slot, slot, b_send.at[i, n], b_recv.at[i, n], (b_next, b_prev)[i], rep)

    def b2_copy(j, k):
        i = k % 2
        slot = ring.at[m4(b0 + (-1, 1)[i]), m4(a0 + place(j)), zs[k]]
        n = j * 4 + k
        return remote(slot, slot, b2_send.at[n], b2_recv.at[n], (b_next, b_prev)[i], rep)

    def b2_arrival(j, k):
        slot = ring.at[m4(b0 + 2), m4(a0 + place(j)), zs[k]]
        n = j * 4 + k
        return remote(slot, slot, b2_send.at[n], b2_recv.at[n], (b_next, b_prev)[k % 2], rep)

    def s_copy(h, j, k):
        bb, aa = m4(b0 + place(h)), m4(a0 + place(j))
        n = h * 16 + j * 4 + k
        return remote(
            ring.at[bb, aa, zs[k]], sib.at[bb, aa, zs[k]], s_send.at[n], s_recv.at[n], seq, mate
        )

    def s_arrival(h, j, k):
        bb, aa = m4(a0 + place(h)), m4(b0 + place(j))
        n = h * 16 + j * 4 + k
        return remote(
            ring.at[bb, aa, zs[k]], sib.at[bb, aa, zs[k]], s_send.at[n], s_recv.at[n], seq, mate
        )

    lane = lax.broadcasted_iota(jnp.int32, (1, 4 * HALF), 1)
    zblock = (
        jnp.where(lane >= HALF, 1, 0)
        + jnp.where(lane >= 2 * HALF, 1, 0)
        + jnp.where(lane >= 3 * HALF, 1, 0)
    )
    within = lane - HALF * zblock
    qrow = lax.broadcasted_iota(jnp.int32, (q_ref.shape[0], 1), 0)
    qpos = qrow - jnp.where(qrow >= span_rows, span_rows, 0) + seq * span_rows

    def attend(buf, b, a, stride_a, stride_b, half):
        keys = buf[b, a].reshape(4 * HALF, KEYW)
        row = within + half * HALF
        owner = a * stride_a + b * stride_b + zblock * 4
        kpos = jnp.where(row < prior_rows, -1, owner * span_rows + row - prior_rows)
        s = lax.dot_general(
            q_ref[...], keys, (((1,), (1,)), ((), ())), preferred_element_type=jnp.float32
        )
        s = jnp.where(kpos <= qpos, s * scale, -1e30)
        m_old = mx[:, :1]
        m_new = jnp.maximum(m_old, jnp.max(s, axis=1, keepdims=True))
        alpha = jnp.exp(m_old - m_new)
        p = jnp.exp(s - m_new)
        sm[...] = sm[...] * alpha + jnp.sum(p, axis=1, keepdims=True)
        mx[...] = jnp.broadcast_to(m_new, mx.shape)
        acc[...] = acc[...] * alpha + jnp.dot(
            p.astype(jnp.bfloat16), keys[:, :LATW], preferred_element_type=jnp.float32
        )

    def attend_ring(h, j):
        attend(ring, m4(b0 + place(h)), m4(a0 + place(j)), sa, sb, core)

    def attend_sib(h, j):
        attend(sib, m4(a0 + place(h)), m4(b0 + place(j)), sb, sa, 1 - core)

    for k in range(3):
        z_copy(k).start()
    for i in range(2):
        a_copy(i, 0).start()
        b_copy(i, 0, 0).start()
    for k in (1, 2, 3):
        z_arrival(k - 1).wait_recv()
        for i in range(2):
            a_copy(i, k).start()
        for i in range(2):
            b_copy(i, 0, k).start()
        s_copy(0, 0, k).start()
    for k in range(4):
        for i in range(2):
            a_arrival(i, k).wait_recv()
            if k % 2 == i:
                a2_copy(k).start()
            j = (2, 1)[i]
            b_copy(0, j, k).start()
            b_copy(1, j, k).start()
            s_copy(0, j, k).start()
    attend_ring(0, 0)
    for k in range(4):
        a2_arrival(k).wait_recv()
        b_copy(0, 3, k).start()
        b_copy(1, 3, k).start()
        s_copy(0, 3, k).start()
    for k in (1, 2, 3):
        s_arrival(0, 0, k).wait_recv()
    attend_sib(0, 0)

    def first_b(j, carry):
        for k in range(4):
            for i in range(2):
                b_arrival(i, j, k).wait_recv()
                if k % 2 == i:
                    b2_copy(j, k).start()
                s_copy((2, 1)[i], j, k).start()
        attend_ring(1, j)
        attend_ring(2, j)
        return carry

    def column(j, carry):
        for k in range(4):
            s_arrival(0, j, k).wait_recv()
        attend_ring(0, j)
        attend_sib(0, j)
        return carry

    def first_b_sib(j, carry):
        for h in (1, 2):
            for k in range(4):
                s_arrival(h, j, k).wait_recv()
            attend_sib(h, j)
        return carry

    def last_b(j, carry):
        for k in range(4):
            b2_arrival(j, k).wait_recv()
            s_copy(3, j, k).start()
        attend_ring(3, j)
        return carry

    def last_sib(j, carry):
        for k in range(4):
            s_arrival(3, j, k).wait_recv()
        attend_sib(3, j)
        return carry

    def middle(j, carry):
        column(j, carry)
        first_b(j, carry)
        return carry

    first_b(0, 0)
    lax.fori_loop(1, 4, middle, 0)

    def closing(j, carry):
        first_b_sib(j, carry)
        last_b(j, carry)
        return carry

    lax.fori_loop(0, 4, closing, 0)
    lax.fori_loop(0, 4, last_sib, 0)
    out_ref[...] = (acc[...] / sm[:, :1]).astype(out_ref.dtype)

    for k in range(3):
        z_copy(k).wait_send()
    for k in range(4):
        for i in range(2):
            a_copy(i, k).wait_send()
        a2_copy(k).wait_send()

    def drain(j, carry):
        for k in range(4):
            for i in range(2):
                b_copy(i, j, k).wait_send()
            b2_copy(j, k).wait_send()
            for h in (1, 2, 3):
                s_copy(h, j, k).wait_send()
        return carry

    lax.fori_loop(0, 4, drain, 0)
    for k in (1, 2, 3):
        s_copy(0, 0, k).wait_send()

    def drain_column(j, carry):
        for k in range(4):
            s_copy(0, j, k).wait_send()
        return carry

    lax.fori_loop(1, 4, drain_column, 0)


def gathered_attention(queries, own_keys, scale, prior_rows, span_rows):
    rows = queries.shape[0]
    dma = pltpu.SemaphoreType.DMA
    return pl.pallas_call(
        functools.partial(attend_kernel, scale, prior_rows, span_rows),
        out_shape=jax.ShapeDtypeStruct((rows, LATW), jnp.bfloat16),
        in_specs=[pl.BlockSpec(memory_space=pltpu.VMEM)] * 2,
        out_specs=pl.BlockSpec(memory_space=pltpu.VMEM),
        scratch_shapes=[
            pltpu.VMEM((4, 4, 4, HALF, KEYW), jnp.bfloat16),
            pltpu.VMEM((4, 4, 4, HALF, KEYW), jnp.bfloat16),
            pltpu.VMEM((rows, LATW), jnp.float32),
            pltpu.VMEM((rows, 128), jnp.float32),
            pltpu.VMEM((rows, 128), jnp.float32),
            dma((2,)),
            dma((3,)),
            dma((3,)),
            dma((2, 4)),
            dma((2, 4)),
            dma((4,)),
            dma((4,)),
            dma((2, 16)),
            dma((2, 16)),
            dma((16,)),
            dma((16,)),
            dma((64,)),
            dma((64,)),
        ],
        name="gather_attend",
        compiler_params=pltpu.CompilerParams(
            collective_id=0, has_side_effects=True, vmem_limit_bytes=40 << 20
        ),
    )(queries, own_keys)


def on_device(
    tokens,
    prior_cache,
    attn_gain,
    q_weight,
    kv_weight,
    kv_gain,
    key_up,
    value_up,
    out_weight,
    moe_gain,
    router,
    expert_ids,
    w_gate,
    w_up,
    w_down,
    handover,
    lengths,
    request_owner,
    page_table,
):
    seq_count = lax.axis_size("seq")
    rep_count = lax.axis_size("rep")
    seq_index = lax.axis_index("seq")
    rep_index = lax.axis_index("rep")
    tok_dev = tokens.shape[0]
    quarter = tok_dev // rep_count
    prior_dev = prior_cache.shape[0]
    local_heads = key_up.shape[0]
    nope_width = key_up.shape[1]
    latent_width = key_up.shape[2]
    rope_width = q_weight.shape[1] // local_heads - nope_width
    prior_total = prior_dev * seq_count
    token_float = tokens.astype(jnp.float32)
    normed = rms_scale(token_float, attn_gain).astype(jnp.bfloat16)
    span_pos = seq_index * tok_dev + jnp.arange(tok_dev)
    positions = prior_total + span_pos
    projected = jnp.dot(normed, q_weight, preferred_element_type=jnp.float32).reshape(
        tok_dev, local_heads, nope_width + rope_width
    )
    q_nope = projected[..., :nope_width].astype(jnp.bfloat16)
    q_rope = rotate(projected[..., nope_width:], positions)
    q_latent = jnp.einsum("thn,hnc->htc", q_nope, key_up, preferred_element_type=jnp.float32)
    queries = (
        jnp.concatenate([q_latent, jnp.transpose(q_rope, (1, 0, 2))], axis=2)
        .astype(jnp.bfloat16)
        .reshape(local_heads * tok_dev, latent_width + rope_width)
    )
    score_scale = (nope_width + rope_width) ** (-0.5)
    block_keys = jnp.concatenate(
        [prior_cache, latent_keys(normed, positions, kv_weight, kv_gain, latent_width)], axis=0
    )
    spare = KEYW - latent_width - rope_width
    head_latent = gathered_attention(
        jnp.pad(queries, ((0, 0), (0, spare))),
        jnp.pad(block_keys, ((0, 0), (0, spare))),
        score_scale,
        prior_dev,
        tok_dev,
    ).reshape(local_heads, tok_dev, latent_width)
    heads_out = (
        jnp.einsum("htc,hcv->thv", head_latent, value_up, preferred_element_type=jnp.float32)
        .astype(jnp.bfloat16)
        .reshape(tok_dev, -1)
    )
    head_partial = jnp.dot(heads_out, out_weight, preferred_element_type=jnp.float32)
    experts_total = router.shape[1]
    local_experts = w_gate.shape[0]
    top_count = expert_ids.shape[1]
    capacity = max(2, min(quarter, 4 * quarter * top_count // (3 * experts_total)))
    slot_count = experts_total * capacity
    target = slot_table(expert_ids.reshape(rep_count, quarter, top_count), experts_total, capacity)
    own_target = lax.dynamic_index_in_dim(target, rep_index, 0, keepdims=False)
    model_width = tokens.shape[1]
    attention = sent_and_summed(head_partial.astype(jnp.bfloat16), "rep", 0)
    hidden_own = lax.dynamic_slice_in_dim(token_float, rep_index * quarter, quarter, 0) + attention
    moe_own = rms_scale(hidden_own, moe_gain).astype(jnp.bfloat16)
    rows_from, live_mask = source_rows(own_target[None, :], slot_count)
    token_of = (rows_from // top_count).reshape(1, experts_total, capacity).transpose(1, 0, 2)
    live_mask = live_mask.reshape(1, experts_total, capacity).transpose(1, 0, 2)
    outgoing = jnp.where(
        live_mask[..., None] > 0, jnp.take(moe_own, token_of, axis=0), jnp.zeros((), jnp.bfloat16)
    )
    group_size = handover.shape[0]
    req_dev = group_size // seq_count
    owner_here = lax.dynamic_slice_in_dim(request_owner, rep_index * group_size, group_size, 0)
    request_index = jnp.arange(group_size)
    earlier = jnp.sum(
        (
            (owner_here[None, :] == owner_here[:, None])
            & (request_index[None, :] < request_index[:, None])
        ).astype(jnp.int32),
        axis=1,
    )
    order_key = owner_here * req_dev + earlier
    picked = jnp.argmax((order_key[None, :] == request_index[:, None]).astype(jnp.int32), axis=1)
    parcel = jnp.take(handover, picked, axis=0)
    arrived, parcels = (
        lax.all_to_all(outgoing, "seq", split_axis=0, concat_axis=0, tiled=True),
        lax.all_to_all(parcel, "seq", split_axis=0, concat_axis=0, tiled=True),
    )
    expert_rows = arrived.reshape(
        seq_count, local_experts, outgoing.shape[1], capacity, model_width
    )
    expert_rows = lax.all_gather(expert_rows, "rep", axis=2, tiled=True)
    gate_sum = jnp.einsum(
        "slqcd,ldf->slqcf", expert_rows, w_gate, preferred_element_type=jnp.float32
    )
    up_sum = jnp.einsum("slqcd,ldf->slqcf", expert_rows, w_up, preferred_element_type=jnp.float32)
    activated = (jax.nn.silu(gate_sum) * up_sum).astype(jnp.bfloat16)
    expert_out = jnp.einsum(
        "slqcf,lfd->slqcd", activated, w_down, preferred_element_type=jnp.float32
    )
    expert_share = lax.psum_scatter(
        expert_out.astype(jnp.bfloat16), "rep", scatter_dimension=2, tiled=True
    )
    returned = lax.all_to_all(expert_share, "seq", split_axis=0, concat_axis=0, tiled=True).reshape(
        slot_count, model_width
    )
    own_ids = lax.dynamic_slice_in_dim(expert_ids, rep_index * quarter, quarter, 0)
    logits = jnp.dot(moe_own, router, preferred_element_type=jnp.float32)
    chosen = jnp.take_along_axis(logits, own_ids, axis=1)
    gate_score = jax.nn.sigmoid(chosen)
    weights = route_scale * gate_score / jnp.sum(gate_score, axis=1, keepdims=True)
    gathered = jnp.take(returned, own_target, axis=0).reshape(quarter, top_count, model_width)
    moe_sum = jnp.sum(weights[..., None] * gathered.astype(jnp.float32), axis=1)
    layer_out = (hidden_own + moe_sum).astype(jnp.bfloat16)
    layers_here = handover.shape[1]
    pos_dev = handover.shape[2]
    row_width = handover.shape[3]
    maxlen = seq_count * pos_dev
    pages_per = maxlen // PAGE
    stacked = (
        parcels.reshape(seq_count, req_dev, layers_here, pos_dev, row_width)
        .transpose(1, 2, 0, 3, 4)
        .reshape(req_dev, layers_here, maxlen, row_width)
    )
    own_requests = (
        lax.dynamic_slice_in_dim(picked, seq_index * req_dev, req_dev, 0) + rep_index * group_size
    )
    own_lengths = jnp.take(lengths, own_requests)
    alive_mask = jnp.arange(maxlen)[None, :] < own_lengths[:, None]
    stacked = jnp.where(alive_mask[:, None, :, None], stacked, jnp.zeros((), jnp.bfloat16))
    page_rows = (
        stacked.reshape(req_dev, layers_here, pages_per, PAGE, row_width)
        .transpose(0, 2, 1, 3, 4)
        .reshape(req_dev * pages_per, layers_here, PAGE, row_width)
    )
    physical = jnp.take(page_table, own_requests, axis=0).reshape(-1)
    inverse = jnp.argmax(
        (physical[None, :] == jnp.arange(req_dev * pages_per)[:, None]).astype(jnp.int32), axis=1
    )
    decode_pages = jnp.take(page_rows, inverse, axis=0)
    return (layer_out, decode_pages)


def solution(mesh):
    return jax.shard_map(
        on_device,
        mesh=mesh,
        in_specs=(
            P("seq", None),
            P("seq", None),
            P(),
            P(None, "rep"),
            P(),
            P(),
            P("rep", None, None),
            P("rep", None, None),
            P("rep", None),
            P(),
            P(),
            P("seq", None),
            P("seq", None, "rep"),
            P("seq", None, "rep"),
            P("seq", "rep", None),
            P("rep", None, "seq", None),
            P(),
            P(),
            P(),
        ),
        out_specs=(P(("seq", "rep"), None), P(("seq", "rep"), None, None, None)),
        check_vma=False,
    )
```

```python
import functools
import jax
import jax.numpy as jnp
from jax import lax
from jax.experimental import pallas as pl
from jax.experimental.pallas import tpu as pltpu
from jax.sharding import PartitionSpec as P

PAGE = 128
MESH = pl.DeviceIdType.MESH
HALF = 80
LATW = 512
KEYW = 640


epsilon = 1e-06
rope_base = 50000.0
route_scale = 2.446


def cut_along(value, dim, peers):
    lengths = value.shape
    pieces = value.reshape(*lengths[:dim], peers, lengths[dim] // peers, *lengths[dim + 1 :])
    return jnp.moveaxis(pieces, dim, 0)


def sent_and_summed(value, axis, dim):
    pieces = cut_along(value, dim, lax.axis_size(axis))
    arrived = lax.all_to_all(pieces, axis, split_axis=0, concat_axis=0, tiled=True)
    return arrived.astype(jnp.float32).sum(axis=0)


def rms_scale(values, gain_vector):
    return (
        values
        * lax.rsqrt(jnp.mean(values * values, axis=-1, keepdims=True) + epsilon)
        * gain_vector
    )


def rotate(values, positions):
    half_width = values.shape[-1] // 2
    frequency = rope_base ** (-jnp.arange(half_width).astype(jnp.float32) / half_width)
    angles = (
        positions.astype(jnp.float32).reshape((-1,) + (1,) * (values.ndim - 2) + (1,)) * frequency
    )
    cosine = jnp.cos(angles)
    sine_values = jnp.sin(angles)
    front_half = values[..., :half_width]
    back_half = values[..., half_width:]
    return jnp.concatenate(
        [
            front_half * cosine - back_half * sine_values,
            back_half * cosine + front_half * sine_values,
        ],
        axis=-1,
    )


def latent_keys(row_block, positions, kv_weight, kv_gain, latent_width):
    latent = jnp.dot(row_block, kv_weight, preferred_element_type=jnp.float32)
    return jnp.concatenate(
        [rms_scale(latent[:, :latent_width], kv_gain), rotate(latent[:, latent_width:], positions)],
        axis=1,
    ).astype(jnp.bfloat16)


def remote(src, dst, send_sem, recv_sem, seq, rep):
    return pltpu.make_async_remote_copy(
        src_ref=src,
        dst_ref=dst,
        send_sem=send_sem,
        recv_sem=recv_sem,
        device_id=(seq, rep),
        device_id_type=MESH,
    )


def greet(partners):
    barrier = pltpu.get_barrier_semaphore()
    for seq, rep in partners:
        pl.semaphore_signal(barrier, inc=1, device_id=(seq, rep), device_id_type=MESH)
    pl.semaphore_wait(barrier, len(partners))


def ring_offset(j):
    return j + jnp.where(j >= 2, 1, 0) - jnp.where(j >= 3, 2, 0)


def attend_kernel(
    scale,
    prior_rows,
    span_rows,
    q_ref,
    own_ref,
    out_ref,
    ring,
    sib,
    acc,
    mx,
    sm,
    local_sem,
    z_send,
    z_recv,
    a_send,
    a_recv,
    a2_send,
    a2_recv,
    b_send,
    b_recv,
    b2_send,
    b2_recv,
    s_send,
    s_recv,
):
    seq = lax.axis_index("seq")
    rep = lax.axis_index("rep")
    core = lax.rem(rep, 2)
    zl = rep // 2
    x0 = seq // 16
    g = lax.rem(seq // 4, 4)
    y0 = lax.rem(seq, 4)
    a0 = x0 + core * (y0 - x0)
    b0 = y0 + core * (x0 - y0)
    sa = 16 - 15 * core
    sb = 1 + 15 * core
    d = 2 * zl - 1
    mate = rep + 1 - 2 * core
    other = rep + 2 - 4 * zl

    def m4(v):
        return lax.rem(v + 4, 4)

    def seq_of(a, z, b):
        return a * sa + z * 4 + b * sb

    a_next = seq_of(m4(a0 + 1), g, b0)
    a_prev = seq_of(m4(a0 - 1), g, b0)
    b_next = seq_of(a0, g, m4(b0 + 1))
    b_prev = seq_of(a0, g, m4(b0 - 1))
    z_to = [
        (seq_of(a0, m4(g + d), b0), other),
        (seq_of(a0, m4(g + d), b0), rep),
        (seq_of(a0, m4(g + 2), b0), other),
    ]
    z_in = [m4(g + d), m4(g - d), m4(g + 2)]
    partners = [
        (a_next, rep),
        (a_prev, rep),
        (b_next, rep),
        (b_prev, rep),
        (seq, mate),
        z_to[0],
        z_to[1],
        (seq_of(a0, m4(g - d), b0), rep),
        z_to[2],
    ]
    zs = [g] + z_in

    def place(j):
        return ring_offset(j)

    own_slot = ring.at[b0, a0, g]
    local = pltpu.make_async_copy(
        own_ref.at[pl.ds(pl.multiple_of(core * HALF, HALF), HALF)], own_slot, local_sem.at[0]
    )
    local_sib = pltpu.make_async_copy(
        own_ref.at[pl.ds(pl.multiple_of((1 - core) * HALF, HALF), HALF)],
        sib.at[a0, b0, g],
        local_sem.at[1],
    )
    local.start()
    local_sib.start()
    mx[...] = jnp.full(mx.shape, -1e30, jnp.float32)
    sm[...] = jnp.zeros(sm.shape, jnp.float32)
    acc[...] = jnp.zeros(acc.shape, jnp.float32)
    local.wait()
    local_sib.wait()
    greet(partners)

    def z_copy(k):
        return remote(own_slot, own_slot, z_send.at[k], z_recv.at[k], z_to[k][0], z_to[k][1])

    def z_arrival(k):
        slot = ring.at[b0, a0, z_in[k]]
        return remote(slot, slot, z_send.at[k], z_recv.at[k], z_to[k][0], z_to[k][1])

    def a_copy(i, k):
        slot = ring.at[b0, a0, zs[k]]
        return remote(slot, slot, a_send.at[i, k], a_recv.at[i, k], (a_next, a_prev)[i], rep)

    def a_arrival(i, k):
        slot = ring.at[b0, m4(a0 + (-1, 1)[i]), zs[k]]
        return remote(slot, slot, a_send.at[i, k], a_recv.at[i, k], (a_next, a_prev)[i], rep)

    def a2_copy(k):
        i = k % 2
        slot = ring.at[b0, m4(a0 + (-1, 1)[i]), zs[k]]
        return remote(slot, slot, a2_send.at[k], a2_recv.at[k], (a_next, a_prev)[i], rep)

    def a2_arrival(k):
        slot = ring.at[b0, m4(a0 + 2), zs[k]]
        return remote(slot, slot, a2_send.at[k], a2_recv.at[k], (a_next, a_prev)[k % 2], rep)

    def b_copy(i, j, k):
        slot = ring.at[b0, m4(a0 + place(j)), zs[k]]
        n = j * 4 + k
        return remote(slot, slot, b_send.at[i, n], b_recv.at[i, n], (b_next, b_prev)[i], rep)

    def b_arrival(i, j, k):
        slot = ring.at[m4(b0 + (-1, 1)[i]), m4(a0 + place(j)), zs[k]]
        n = j * 4 + k
        return remote(slot, slot, b_send.at[i, n], b_recv.at[i, n], (b_next, b_prev)[i], rep)

    def b2_copy(j, k):
        i = k % 2
        slot = ring.at[m4(b0 + (-1, 1)[i]), m4(a0 + place(j)), zs[k]]
        n = j * 4 + k
        return remote(slot, slot, b2_send.at[n], b2_recv.at[n], (b_next, b_prev)[i], rep)

    def b2_arrival(j, k):
        slot = ring.at[m4(b0 + 2), m4(a0 + place(j)), zs[k]]
        n = j * 4 + k
        return remote(slot, slot, b2_send.at[n], b2_recv.at[n], (b_next, b_prev)[k % 2], rep)

    def s_copy(h, j, k):
        bb, aa = m4(b0 + place(h)), m4(a0 + place(j))
        n = h * 16 + j * 4 + k
        return remote(
            ring.at[bb, aa, zs[k]], sib.at[bb, aa, zs[k]], s_send.at[n], s_recv.at[n], seq, mate
        )

    def s_arrival(h, j, k):
        bb, aa = m4(a0 + place(h)), m4(b0 + place(j))
        n = h * 16 + j * 4 + k
        return remote(
            ring.at[bb, aa, zs[k]], sib.at[bb, aa, zs[k]], s_send.at[n], s_recv.at[n], seq, mate
        )

    lane = lax.broadcasted_iota(jnp.int32, (1, 4 * HALF), 1)
    zblock = (
        jnp.where(lane >= HALF, 1, 0)
        + jnp.where(lane >= 2 * HALF, 1, 0)
        + jnp.where(lane >= 3 * HALF, 1, 0)
    )
    within = lane - HALF * zblock
    qrow = lax.broadcasted_iota(jnp.int32, (q_ref.shape[0], 1), 0)
    qpos = qrow - jnp.where(qrow >= span_rows, span_rows, 0) + seq * span_rows

    def attend(buf, b, a, stride_a, stride_b, half):
        keys = buf[b, a].reshape(4 * HALF, KEYW)
        row = within + half * HALF
        owner = a * stride_a + b * stride_b + zblock * 4
        kpos = jnp.where(row < prior_rows, -1, owner * span_rows + row - prior_rows)
        s = lax.dot_general(
            q_ref[...], keys, (((1,), (1,)), ((), ())), preferred_element_type=jnp.float32
        )
        s = jnp.where(kpos <= qpos, s * scale, -1e30)
        m_old = mx[:, :1]
        m_new = jnp.maximum(m_old, jnp.max(s, axis=1, keepdims=True))
        alpha = jnp.exp(m_old - m_new)
        p = jnp.exp(s - m_new)
        sm[...] = sm[...] * alpha + jnp.sum(p, axis=1, keepdims=True)
        mx[...] = jnp.broadcast_to(m_new, mx.shape)
        acc[...] = acc[...] * alpha + jnp.dot(
            p.astype(jnp.bfloat16), keys[:, :LATW], preferred_element_type=jnp.float32
        )

    def attend_ring(h, j):
        attend(ring, m4(b0 + place(h)), m4(a0 + place(j)), sa, sb, core)

    def attend_sib(h, j):
        attend(sib, m4(a0 + place(h)), m4(b0 + place(j)), sb, sa, 1 - core)

    for k in range(3):
        z_copy(k).start()
    for i in range(2):
        a_copy(i, 0).start()
        b_copy(i, 0, 0).start()
    for k in (1, 2, 3):
        z_arrival(k - 1).wait_recv()
        for i in range(2):
            a_copy(i, k).start()
        for i in range(2):
            b_copy(i, 0, k).start()
        s_copy(0, 0, k).start()
    for k in range(4):
        for i in range(2):
            a_arrival(i, k).wait_recv()
            if k % 2 == i:
                a2_copy(k).start()
            j = (2, 1)[i]
            b_copy(0, j, k).start()
            b_copy(1, j, k).start()
            s_copy(0, j, k).start()
    attend_ring(0, 0)
    for k in range(4):
        a2_arrival(k).wait_recv()
        b_copy(0, 3, k).start()
        b_copy(1, 3, k).start()
        s_copy(0, 3, k).start()
    for k in (1, 2, 3):
        s_arrival(0, 0, k).wait_recv()
    attend_sib(0, 0)

    def first_b(j, carry):
        for k in range(4):
            for i in range(2):
                b_arrival(i, j, k).wait_recv()
                if k % 2 == i:
                    b2_copy(j, k).start()
                s_copy((2, 1)[i], j, k).start()
        attend_ring(1, j)
        attend_ring(2, j)
        return carry

    def column(j, carry):
        for k in range(4):
            s_arrival(0, j, k).wait_recv()
        attend_ring(0, j)
        attend_sib(0, j)
        return carry

    def first_b_sib(j, carry):
        for h in (1, 2):
            for k in range(4):
                s_arrival(h, j, k).wait_recv()
            attend_sib(h, j)
        return carry

    def last_b(j, carry):
        for k in range(4):
            b2_arrival(j, k).wait_recv()
            s_copy(3, j, k).start()
        attend_ring(3, j)
        return carry

    def last_sib(j, carry):
        for k in range(4):
            s_arrival(3, j, k).wait_recv()
        attend_sib(3, j)
        return carry

    def middle(j, carry):
        column(j, carry)
        first_b(j, carry)
        return carry

    first_b(0, 0)
    lax.fori_loop(1, 4, middle, 0)

    def closing(j, carry):
        first_b_sib(j, carry)
        last_b(j, carry)
        return carry

    lax.fori_loop(0, 4, closing, 0)
    lax.fori_loop(0, 4, last_sib, 0)
    out_ref[...] = (acc[...] / sm[:, :1]).astype(out_ref.dtype)

    for k in range(3):
        z_copy(k).wait_send()
    for k in range(4):
        for i in range(2):
            a_copy(i, k).wait_send()
        a2_copy(k).wait_send()

    def drain(j, carry):
        for k in range(4):
            for i in range(2):
                b_copy(i, j, k).wait_send()
            b2_copy(j, k).wait_send()
            for h in (1, 2, 3):
                s_copy(h, j, k).wait_send()
        return carry

    lax.fori_loop(0, 4, drain, 0)
    for k in (1, 2, 3):
        s_copy(0, 0, k).wait_send()

    def drain_column(j, carry):
        for k in range(4):
            s_copy(0, j, k).wait_send()
        return carry

    lax.fori_loop(1, 4, drain_column, 0)


def gathered_attention(queries, own_keys, scale, prior_rows, span_rows):
    rows = queries.shape[0]
    dma = pltpu.SemaphoreType.DMA
    return pl.pallas_call(
        functools.partial(attend_kernel, scale, prior_rows, span_rows),
        out_shape=jax.ShapeDtypeStruct((rows, LATW), jnp.bfloat16),
        in_specs=[pl.BlockSpec(memory_space=pltpu.VMEM)] * 2,
        out_specs=pl.BlockSpec(memory_space=pltpu.VMEM),
        scratch_shapes=[
            pltpu.VMEM((4, 4, 4, HALF, KEYW), jnp.bfloat16),
            pltpu.VMEM((4, 4, 4, HALF, KEYW), jnp.bfloat16),
            pltpu.VMEM((rows, LATW), jnp.float32),
            pltpu.VMEM((rows, 128), jnp.float32),
            pltpu.VMEM((rows, 128), jnp.float32),
            dma((2,)),
            dma((3,)),
            dma((3,)),
            dma((2, 4)),
            dma((2, 4)),
            dma((4,)),
            dma((4,)),
            dma((2, 16)),
            dma((2, 16)),
            dma((16,)),
            dma((16,)),
            dma((64,)),
            dma((64,)),
        ],
        name="gather_attend",
        compiler_params=pltpu.CompilerParams(
            collective_id=0, has_side_effects=True, vmem_limit_bytes=40 << 20
        ),
    )(queries, own_keys)


SLOTS = 4
BLOCK = 32


def expert_kernel(
    rows_ref,
    hidden_ref,
    wg_hbm,
    wu_hbm,
    wd_hbm,
    out_ref,
    toks,
    wg,
    wu,
    wd,
    outb,
    xin,
    kept,
    ysend,
    yrecv,
    back,
    got,
    part,
    fsend,
    frecv,
    bsend,
    brecv,
    w_sem,
    l_sem,
    agf_send,
    agf_recv,
    agb_send,
    agb_recv,
    d_send,
    d_recv,
    s_send,
    s_recv,
    y_send,
    y_recv,
    r_send,
    r_recv,
    f_send,
    f_recv,
    b_send,
    b_recv,
):
    seq = lax.axis_index("seq")
    rep = lax.axis_index("rep")
    core = lax.rem(rep, 2)
    zc = lax.rem(seq // 4, 4) * 2 + rep // 2
    zhi = lax.rem(seq // 4, 4)
    x0 = seq // 16
    y0 = lax.rem(seq, 4)
    here = x0 * 4 + y0
    way = 1 - 2 * core
    mate = rep + 1 - 2 * core
    width = hidden_ref.shape[1]

    def chip(z):
        z = lax.rem(z + 8, 8)
        return x0 * 16 + (z // 2) * 4 + y0, lax.rem(z, 2) * 2 + core

    ahead = chip(zc + way)
    behind = chip(zc - way)

    def to_peer(p):
        return lax.rem(x0 + p // 4, 4), lax.rem(y0 + lax.rem(p, 4), 4)

    def from_peer(p):
        return lax.rem(x0 + 4 - p // 4, 4), lax.rem(y0 + 4 - lax.rem(p, 4), 4)

    def plane_seq(xy):
        return xy[0] * 16 + zhi * 4 + xy[1]

    partners = [ahead, behind, (seq, mate)] + [(plane_seq(to_peer(p)), rep) for p in range(1, 16)]

    w_copies = [
        pltpu.make_async_copy(wg_hbm.at[0], wg, w_sem.at[0]),
        pltpu.make_async_copy(wu_hbm.at[0], wu, w_sem.at[1]),
        pltpu.make_async_copy(wd_hbm.at[0], wd, w_sem.at[2]),
    ]
    for copy in w_copies:
        copy.start()
    first = pltpu.make_async_copy(rows_ref, toks.at[0], l_sem.at[0])
    first.start()
    first.wait()
    greet(partners)

    def agf(k):
        source = (0, 1, 3, 5)[k]
        return remote(
            toks.at[source], toks.at[2 * k + 1], agf_send.at[k], agf_recv.at[k], ahead[0], ahead[1]
        )

    def agb(k):
        source = (0, 2, 4)[k]
        return remote(
            toks.at[source], toks.at[2 * k + 2], agb_send.at[k], agb_recv.at[k], behind[0], behind[1]
        )

    lane = lax.broadcasted_iota(jnp.int32, (1, 256), 1)
    code = (
        (((lane >> 6) * 16) + zhi * 4 + ((lane >> 4) & 3)) * SLOTS + (lane & 3)
    ).astype(jnp.float32)
    lane_block = (lane >> 2) & 3
    token_block = lax.broadcasted_iota(jnp.int32, (128, 1), 0) >> 5
    same_block = token_block == lane_block

    def tokens_of(ph):
        return toks[4 * ph : 4 * ph + 4].reshape(128, width + 128)

    def dispatch_copy(ph, p):
        xy = to_peer(p)
        return remote(
            outb.at[ph, xy[0] * 4 + xy[1]],
            xin.at[core, ph, here],
            d_send.at[ph, p],
            d_recv.at[ph, p],
            plane_seq(xy),
            rep,
        )

    def own_rows(ph):
        return pltpu.make_async_copy(
            outb.at[ph, here], xin.at[core, ph, here], l_sem.at[1 + ph]
        )

    def share(ph, p):
        xy = from_peer(p)
        slot = xin.at[core, ph, xy[0] * 4 + xy[1]]
        return remote(slot, slot, s_send.at[ph, p], s_recv.at[ph, p], seq, mate)

    def share_arrival(ph, p):
        xy = from_peer(p)
        slot = xin.at[1 - core, ph, xy[0] * 4 + xy[1]]
        return remote(slot, slot, s_send.at[ph, p], s_recv.at[ph, p], seq, mate)

    def dispatch(ph):
        block = tokens_of(ph)
        meta = block[:, width:].astype(jnp.float32)
        hit = meta[:, 0:1] == code
        for k in range(1, 6):
            hit = hit | (meta[:, k : k + 1] == code)
        pick = jnp.where(hit & same_block, 1.0, 0.0).astype(jnp.bfloat16)
        rows = lax.dot_general(
            pick, block[:, :width], (((0,), (0,)), ((), ())), preferred_element_type=jnp.float32
        )
        outb[ph] = rows.astype(jnp.bfloat16).reshape(16, 16, width)

        def send(p, carry):
            dispatch_copy(ph, p).start()
            return carry

        lax.fori_loop(1, 16, send, 0)
        own_rows(ph).start()

    def arrivals(ph):
        own_rows(ph).wait()
        share(ph, 0).start()

        def one(p, carry):
            dispatch_copy(ph, p).wait_recv()
            share(ph, p).start()
            return carry

        lax.fori_loop(1, 16, one, 0)

    def share_arrivals(ph):
        def one(p, carry):
            share_arrival(ph, p).wait_recv()
            return carry

        lax.fori_loop(0, 16, one, 0)

    def expert(which, ph):
        rows = xin[which, ph].reshape(256, width)
        gate = jnp.dot(rows, wg[...], preferred_element_type=jnp.float32)
        up = jnp.dot(rows, wu[...], preferred_element_type=jnp.float32)
        act = (jax.nn.silu(gate) * up).astype(jnp.bfloat16)
        return jnp.dot(act, wd[...], preferred_element_type=jnp.float32)

    def pair_copy(ph):
        return remote(ysend.at[ph], yrecv.at[ph], y_send.at[ph], y_recv.at[ph], seq, mate)

    def return_copy(ph, p):
        xy = to_peer(p)
        return remote(
            back.at[ph, xy[0] * 4 + xy[1]],
            got.at[ph, here],
            r_send.at[ph, p],
            r_recv.at[ph, p],
            plane_seq(xy),
            rep,
        )

    def own_back(ph):
        return pltpu.make_async_copy(back.at[ph, here], got.at[ph, here], l_sem.at[3 + ph])

    def give_back(ph):
        pair_copy(ph).wait_recv()
        total = kept[ph] + yrecv[ph].astype(jnp.float32)
        back[ph] = total.astype(jnp.bfloat16).reshape(16, 16, width)

        def send(p, carry):
            return_copy(ph, p).start()
            return carry

        lax.fori_loop(1, 16, send, 0)
        own_back(ph).start()

    def combine(ph):
        def one(p, carry):
            return_copy(ph, p).wait_recv()
            return carry

        lax.fori_loop(1, 16, one, 0)
        own_back(ph).wait()
        meta = toks[4 * ph : 4 * ph + 4, :, width:].reshape(128, 128).astype(jnp.float32)
        high = jnp.zeros((128, 256), jnp.float32)
        low = jnp.zeros((128, 256), jnp.float32)
        for k in range(6):
            hit = (meta[:, k : k + 1] == code) & same_block
            high = high + jnp.where(hit, meta[:, 6 + k : 7 + k], 0.0)
            low = low + jnp.where(hit, meta[:, 12 + k : 13 + k], 0.0)
        both = jnp.concatenate([high, low], axis=0).astype(jnp.bfloat16)
        sums = jnp.dot(both, got[ph].reshape(256, width), preferred_element_type=jnp.float32)
        part[4 * ph : 4 * ph + 4] = (sums[:128] + sums[128:]).reshape(4, BLOCK, width)

    agf(0).start()
    agb(0).start()
    agf(0).wait_recv()
    agf(1).start()
    agb(0).wait_recv()
    agb(1).start()
    agf(1).wait_recv()
    agf(2).start()
    dispatch(0)
    agb(1).wait_recv()
    agb(2).start()
    agf(2).wait_recv()
    agf(3).start()
    agb(2).wait_recv()
    agf(3).wait_recv()
    dispatch(1)
    for copy in w_copies:
        copy.wait()
    arrivals(0)
    kept[0] = expert(core, 0)
    share_arrivals(0)
    ysend[0] = expert(1 - core, 0).astype(jnp.bfloat16)
    pair_copy(0).start()
    arrivals(1)
    kept[1] = expert(core, 1)
    give_back(0)
    share_arrivals(1)
    ysend[1] = expert(1 - core, 1).astype(jnp.bfloat16)
    pair_copy(1).start()
    give_back(1)
    combine(0)
    combine(1)

    def f_copy(k):
        return remote(fsend.at[k], frecv.at[k], f_send.at[k], f_recv.at[k], ahead[0], ahead[1])

    def b_copy(k):
        return remote(bsend.at[k], brecv.at[k], b_send.at[k], b_recv.at[k], behind[0], behind[1])

    fsend[0] = part[7].astype(jnp.bfloat16)
    f_copy(0).start()
    bsend[0] = part[5].astype(jnp.bfloat16)
    b_copy(0).start()
    for k in range(1, 4):
        f_copy(k - 1).wait_recv()
        fsend[k] = (part[(7, 6, 4, 2)[k]] + frecv[k - 1].astype(jnp.float32)).astype(jnp.bfloat16)
        f_copy(k).start()
        if k < 3:
            b_copy(k - 1).wait_recv()
            bsend[k] = (part[(5, 3, 1)[k]] + brecv[k - 1].astype(jnp.float32)).astype(jnp.bfloat16)
            b_copy(k).start()
    b_copy(2).wait_recv()
    total = hidden_ref[...] + part[0] + brecv[2].astype(jnp.float32)
    f_copy(3).wait_recv()
    out_ref[...] = (total + frecv[3].astype(jnp.float32)).astype(out_ref.dtype)

    for k in range(4):
        agf(k).wait_send()
        f_copy(k).wait_send()
    for k in range(3):
        agb(k).wait_send()
        b_copy(k).wait_send()
    for ph in range(2):
        pair_copy(ph).wait_send()
        share(ph, 0).wait_send()

        def drain(p, carry):
            dispatch_copy(ph, p).wait_send()
            share(ph, p).wait_send()
            return_copy(ph, p).wait_send()
            return carry

        lax.fori_loop(1, 16, drain, 0)


def expert_layer(rows, hidden, w_gate, w_up, w_down):
    width = hidden.shape[1]
    hidden_units = w_gate.shape[2]
    dma = pltpu.SemaphoreType.DMA
    bf16 = jnp.bfloat16
    vmem = pl.BlockSpec(memory_space=pltpu.VMEM)
    anywhere = pl.BlockSpec(memory_space=pl.ANY)
    return pl.pallas_call(
        expert_kernel,
        out_shape=jax.ShapeDtypeStruct(hidden.shape, bf16),
        in_specs=[vmem, vmem, anywhere, anywhere, anywhere],
        out_specs=vmem,
        scratch_shapes=[
            pltpu.VMEM((8, BLOCK, width + 128), bf16),
            pltpu.VMEM((width, hidden_units), bf16),
            pltpu.VMEM((width, hidden_units), bf16),
            pltpu.VMEM((hidden_units, width), bf16),
            pltpu.VMEM((2, 16, 16, width), bf16),
            pltpu.VMEM((2, 2, 16, 16, width), bf16),
            pltpu.VMEM((2, 256, width), jnp.float32),
            pltpu.VMEM((2, 256, width), bf16),
            pltpu.VMEM((2, 256, width), bf16),
            pltpu.VMEM((2, 16, 16, width), bf16),
            pltpu.VMEM((2, 16, 16, width), bf16),
            pltpu.VMEM((8, BLOCK, width), jnp.float32),
            pltpu.VMEM((4, BLOCK, width), bf16),
            pltpu.VMEM((4, BLOCK, width), bf16),
            pltpu.VMEM((3, BLOCK, width), bf16),
            pltpu.VMEM((3, BLOCK, width), bf16),
            dma((3,)),
            dma((5,)),
            dma((4,)),
            dma((4,)),
            dma((3,)),
            dma((3,)),
            dma((2, 16)),
            dma((2, 16)),
            dma((2, 16)),
            dma((2, 16)),
            dma((2,)),
            dma((2,)),
            dma((2, 16)),
            dma((2, 16)),
            dma((4,)),
            dma((4,)),
            dma((3,)),
            dma((3,)),
        ],
        name="experts",
        compiler_params=pltpu.CompilerParams(
            collective_id=1, has_side_effects=True, vmem_limit_bytes=56 << 20
        ),
    )(rows, hidden, w_gate, w_up, w_down)


def on_device(
    tokens,
    prior_cache,
    attn_gain,
    q_weight,
    kv_weight,
    kv_gain,
    key_up,
    value_up,
    out_weight,
    moe_gain,
    router,
    expert_ids,
    w_gate,
    w_up,
    w_down,
    handover,
    lengths,
    request_owner,
    page_table,
):
    seq_count = lax.axis_size("seq")
    rep_count = lax.axis_size("rep")
    seq_index = lax.axis_index("seq")
    rep_index = lax.axis_index("rep")
    tok_dev = tokens.shape[0]
    quarter = tok_dev // rep_count
    prior_dev = prior_cache.shape[0]
    local_heads = key_up.shape[0]
    nope_width = key_up.shape[1]
    latent_width = key_up.shape[2]
    rope_width = q_weight.shape[1] // local_heads - nope_width
    prior_total = prior_dev * seq_count
    token_float = tokens.astype(jnp.float32)
    normed = rms_scale(token_float, attn_gain).astype(jnp.bfloat16)
    span_pos = seq_index * tok_dev + jnp.arange(tok_dev)
    positions = prior_total + span_pos
    projected = jnp.dot(normed, q_weight, preferred_element_type=jnp.float32).reshape(
        tok_dev, local_heads, nope_width + rope_width
    )
    q_nope = projected[..., :nope_width].astype(jnp.bfloat16)
    q_rope = rotate(projected[..., nope_width:], positions)
    q_latent = jnp.einsum("thn,hnc->htc", q_nope, key_up, preferred_element_type=jnp.float32)
    queries = (
        jnp.concatenate([q_latent, jnp.transpose(q_rope, (1, 0, 2))], axis=2)
        .astype(jnp.bfloat16)
        .reshape(local_heads * tok_dev, latent_width + rope_width)
    )
    score_scale = (nope_width + rope_width) ** (-0.5)
    block_keys = jnp.concatenate(
        [prior_cache, latent_keys(normed, positions, kv_weight, kv_gain, latent_width)], axis=0
    )
    spare = KEYW - latent_width - rope_width
    head_latent = gathered_attention(
        jnp.pad(queries, ((0, 0), (0, spare))),
        jnp.pad(block_keys, ((0, 0), (0, spare))),
        score_scale,
        prior_dev,
        tok_dev,
    ).reshape(local_heads, tok_dev, latent_width)
    heads_out = (
        jnp.einsum("htc,hcv->thv", head_latent, value_up, preferred_element_type=jnp.float32)
        .astype(jnp.bfloat16)
        .reshape(tok_dev, -1)
    )
    head_partial = jnp.dot(heads_out, out_weight, preferred_element_type=jnp.float32)
    top_count = expert_ids.shape[1]
    own_ids = lax.dynamic_slice_in_dim(expert_ids, rep_index * quarter, quarter, 0)
    flat_ids = own_ids.reshape(-1)
    flat_index = jnp.arange(flat_ids.shape[0])
    rank = jnp.sum(
        (
            (flat_ids[:, None] == flat_ids[None, :]) & (flat_index[None, :] < flat_index[:, None])
        ).astype(jnp.int32),
        axis=1,
    )
    target = (flat_ids * SLOTS + rank).reshape(quarter, top_count)
    attention = sent_and_summed(head_partial.astype(jnp.bfloat16), "rep", 0)
    hidden_own = lax.dynamic_slice_in_dim(token_float, rep_index * quarter, quarter, 0) + attention
    moe_own = rms_scale(hidden_own, moe_gain).astype(jnp.bfloat16)
    logits = jnp.dot(moe_own, router, preferred_element_type=jnp.float32)
    named = own_ids[:, :, None] == jnp.arange(router.shape[1])[None, None, :]
    chosen = jnp.sum(jnp.where(named, logits[:, None, :], 0.0), axis=2)
    gate_score = jax.nn.sigmoid(chosen)
    weights = route_scale * gate_score / jnp.sum(gate_score, axis=1, keepdims=True)
    high = lax.reduce_precision(weights, 8, 7)
    sent_rows = jnp.concatenate(
        [
            moe_own,
            target.astype(jnp.bfloat16),
            high.astype(jnp.bfloat16),
            (weights - high).astype(jnp.bfloat16),
            jnp.zeros((quarter, 128 - 3 * top_count), jnp.bfloat16),
        ],
        axis=1,
    )
    layer_out = expert_layer(sent_rows, hidden_own, w_gate, w_up, w_down)
    group_size = handover.shape[0]
    req_dev = group_size // seq_count
    owner_here = lax.dynamic_slice_in_dim(request_owner, rep_index * group_size, group_size, 0)
    request_index = jnp.arange(group_size)
    earlier = jnp.sum(
        (
            (owner_here[None, :] == owner_here[:, None])
            & (request_index[None, :] < request_index[:, None])
        ).astype(jnp.int32),
        axis=1,
    )
    order_key = owner_here * req_dev + earlier
    picked = jnp.argmax((order_key[None, :] == request_index[:, None]).astype(jnp.int32), axis=1)
    parcel = jnp.take(handover, picked, axis=0)
    parcels = lax.all_to_all(parcel, "seq", split_axis=0, concat_axis=0, tiled=True)
    layers_here = handover.shape[1]
    pos_dev = handover.shape[2]
    row_width = handover.shape[3]
    maxlen = seq_count * pos_dev
    pages_per = maxlen // PAGE
    stacked = (
        parcels.reshape(seq_count, req_dev, layers_here, pos_dev, row_width)
        .transpose(1, 2, 0, 3, 4)
        .reshape(req_dev, layers_here, maxlen, row_width)
    )
    own_requests = (
        lax.dynamic_slice_in_dim(picked, seq_index * req_dev, req_dev, 0) + rep_index * group_size
    )
    own_lengths = jnp.take(lengths, own_requests)
    alive_mask = jnp.arange(maxlen)[None, :] < own_lengths[:, None]
    stacked = jnp.where(alive_mask[:, None, :, None], stacked, jnp.zeros((), jnp.bfloat16))
    page_rows = (
        stacked.reshape(req_dev, layers_here, pages_per, PAGE, row_width)
        .transpose(0, 2, 1, 3, 4)
        .reshape(req_dev * pages_per, layers_here, PAGE, row_width)
    )
    physical = jnp.take(page_table, own_requests, axis=0).reshape(-1)
    inverse = jnp.argmax(
        (physical[None, :] == jnp.arange(req_dev * pages_per)[:, None]).astype(jnp.int32), axis=1
    )
    decode_pages = jnp.take(page_rows, inverse, axis=0)
    return (layer_out, decode_pages)


def solution(mesh):
    return jax.shard_map(
        on_device,
        mesh=mesh,
        in_specs=(
            P("seq", None),
            P("seq", None),
            P(),
            P(None, "rep"),
            P(),
            P(),
            P("rep", None, None),
            P("rep", None, None),
            P("rep", None),
            P(),
            P(),
            P("seq", None),
            P("seq", None, "rep"),
            P("seq", None, "rep"),
            P("seq", "rep", None),
            P("rep", None, "seq", None),
            P(),
            P(),
            P(),
        ),
        out_specs=(P(("seq", "rep"), None), P(("seq", "rep"), None, None, None)),
        check_vma=False,
    )
```

```python
import functools
import jax
import jax.numpy as jnp
from jax import lax
from jax.experimental import pallas as pl
from jax.experimental.pallas import tpu as pltpu
from jax.sharding import PartitionSpec as P

PAGE = 128
MESH = pl.DeviceIdType.MESH
HALF = 80
LATW = 512
KEYW = 640


epsilon = 1e-06
rope_base = 50000.0
route_scale = 2.446


def cut_along(value, dim, peers):
    lengths = value.shape
    pieces = value.reshape(*lengths[:dim], peers, lengths[dim] // peers, *lengths[dim + 1 :])
    return jnp.moveaxis(pieces, dim, 0)


def sent_and_summed(value, axis, dim):
    pieces = cut_along(value, dim, lax.axis_size(axis))
    arrived = lax.all_to_all(pieces, axis, split_axis=0, concat_axis=0, tiled=True)
    return arrived.astype(jnp.float32).sum(axis=0)


def rms_scale(values, gain_vector):
    return (
        values
        * lax.rsqrt(jnp.mean(values * values, axis=-1, keepdims=True) + epsilon)
        * gain_vector
    )


def rotate(values, positions):
    half_width = values.shape[-1] // 2
    frequency = rope_base ** (-jnp.arange(half_width).astype(jnp.float32) / half_width)
    angles = (
        positions.astype(jnp.float32).reshape((-1,) + (1,) * (values.ndim - 2) + (1,)) * frequency
    )
    cosine = jnp.cos(angles)
    sine_values = jnp.sin(angles)
    front_half = values[..., :half_width]
    back_half = values[..., half_width:]
    return jnp.concatenate(
        [
            front_half * cosine - back_half * sine_values,
            back_half * cosine + front_half * sine_values,
        ],
        axis=-1,
    )


def latent_keys(row_block, positions, kv_weight, kv_gain, latent_width):
    latent = jnp.dot(row_block, kv_weight, preferred_element_type=jnp.float32)
    return jnp.concatenate(
        [rms_scale(latent[:, :latent_width], kv_gain), rotate(latent[:, latent_width:], positions)],
        axis=1,
    ).astype(jnp.bfloat16)


def remote(src, dst, send_sem, recv_sem, seq, rep):
    return pltpu.make_async_remote_copy(
        src_ref=src,
        dst_ref=dst,
        send_sem=send_sem,
        recv_sem=recv_sem,
        device_id=(seq, rep),
        device_id_type=MESH,
    )


def greet(partners):
    barrier = pltpu.get_barrier_semaphore()
    for seq, rep in partners:
        pl.semaphore_signal(barrier, inc=1, device_id=(seq, rep), device_id_type=MESH)
    pl.semaphore_wait(barrier, len(partners))


def ring_offset(j):
    return j + jnp.where(j >= 2, 1, 0) - jnp.where(j >= 3, 2, 0)


def attend_kernel(
    scale,
    prior_rows,
    span_rows,
    q_ref,
    own_ref,
    out_ref,
    ring,
    sib,
    acc,
    mx,
    sm,
    local_sem,
    z_send,
    z_recv,
    a_send,
    a_recv,
    a2_send,
    a2_recv,
    b_send,
    b_recv,
    b2_send,
    b2_recv,
    s_send,
    s_recv,
):
    seq = lax.axis_index("seq")
    rep = lax.axis_index("rep")
    core = lax.rem(rep, 2)
    zl = rep // 2
    x0 = seq // 16
    g = lax.rem(seq // 4, 4)
    y0 = lax.rem(seq, 4)
    a0 = x0 + core * (y0 - x0)
    b0 = y0 + core * (x0 - y0)
    sa = 16 - 15 * core
    sb = 1 + 15 * core
    d = 2 * zl - 1
    mate = rep + 1 - 2 * core
    other = rep + 2 - 4 * zl

    def m4(v):
        return lax.rem(v + 4, 4)

    def seq_of(a, z, b):
        return a * sa + z * 4 + b * sb

    a_next = seq_of(m4(a0 + 1), g, b0)
    a_prev = seq_of(m4(a0 - 1), g, b0)
    b_next = seq_of(a0, g, m4(b0 + 1))
    b_prev = seq_of(a0, g, m4(b0 - 1))
    z_to = [
        (seq_of(a0, m4(g + d), b0), other),
        (seq_of(a0, m4(g + d), b0), rep),
        (seq_of(a0, m4(g + 2), b0), other),
    ]
    z_in = [m4(g + d), m4(g - d), m4(g + 2)]
    partners = [
        (a_next, rep),
        (a_prev, rep),
        (b_next, rep),
        (b_prev, rep),
        (seq, mate),
        z_to[0],
        z_to[1],
        (seq_of(a0, m4(g - d), b0), rep),
        z_to[2],
    ]
    zs = [g] + z_in

    def place(j):
        return ring_offset(j)

    own_slot = ring.at[b0, a0, g]
    local = pltpu.make_async_copy(
        own_ref.at[pl.ds(pl.multiple_of(core * HALF, HALF), HALF)], own_slot, local_sem.at[0]
    )
    local_sib = pltpu.make_async_copy(
        own_ref.at[pl.ds(pl.multiple_of((1 - core) * HALF, HALF), HALF)],
        sib.at[a0, b0, g],
        local_sem.at[1],
    )
    local.start()
    local_sib.start()
    mx[...] = jnp.full(mx.shape, -1e30, jnp.float32)
    sm[...] = jnp.zeros(sm.shape, jnp.float32)
    acc[...] = jnp.zeros(acc.shape, jnp.float32)
    local.wait()
    local_sib.wait()
    greet(partners)

    def z_copy(k):
        return remote(own_slot, own_slot, z_send.at[k], z_recv.at[k], z_to[k][0], z_to[k][1])

    def z_arrival(k):
        slot = ring.at[b0, a0, z_in[k]]
        return remote(slot, slot, z_send.at[k], z_recv.at[k], z_to[k][0], z_to[k][1])

    def a_copy(i, k):
        slot = ring.at[b0, a0, zs[k]]
        return remote(slot, slot, a_send.at[i, k], a_recv.at[i, k], (a_next, a_prev)[i], rep)

    def a_arrival(i, k):
        slot = ring.at[b0, m4(a0 + (-1, 1)[i]), zs[k]]
        return remote(slot, slot, a_send.at[i, k], a_recv.at[i, k], (a_next, a_prev)[i], rep)

    def a2_copy(k):
        i = k % 2
        slot = ring.at[b0, m4(a0 + (-1, 1)[i]), zs[k]]
        return remote(slot, slot, a2_send.at[k], a2_recv.at[k], (a_next, a_prev)[i], rep)

    def a2_arrival(k):
        slot = ring.at[b0, m4(a0 + 2), zs[k]]
        return remote(slot, slot, a2_send.at[k], a2_recv.at[k], (a_next, a_prev)[k % 2], rep)

    def b_copy(i, j, k):
        slot = ring.at[b0, m4(a0 + place(j)), zs[k]]
        n = j * 4 + k
        return remote(slot, slot, b_send.at[i, n], b_recv.at[i, n], (b_next, b_prev)[i], rep)

    def b_arrival(i, j, k):
        slot = ring.at[m4(b0 + (-1, 1)[i]), m4(a0 + place(j)), zs[k]]
        n = j * 4 + k
        return remote(slot, slot, b_send.at[i, n], b_recv.at[i, n], (b_next, b_prev)[i], rep)

    def b2_copy(j, k):
        i = k % 2
        slot = ring.at[m4(b0 + (-1, 1)[i]), m4(a0 + place(j)), zs[k]]
        n = j * 4 + k
        return remote(slot, slot, b2_send.at[n], b2_recv.at[n], (b_next, b_prev)[i], rep)

    def b2_arrival(j, k):
        slot = ring.at[m4(b0 + 2), m4(a0 + place(j)), zs[k]]
        n = j * 4 + k
        return remote(slot, slot, b2_send.at[n], b2_recv.at[n], (b_next, b_prev)[k % 2], rep)

    def s_copy(h, j, k):
        bb, aa = m4(b0 + place(h)), m4(a0 + place(j))
        n = h * 16 + j * 4 + k
        return remote(
            ring.at[bb, aa, zs[k]], sib.at[bb, aa, zs[k]], s_send.at[n], s_recv.at[n], seq, mate
        )

    def s_arrival(h, j, k):
        bb, aa = m4(a0 + place(h)), m4(b0 + place(j))
        n = h * 16 + j * 4 + k
        return remote(
            ring.at[bb, aa, zs[k]], sib.at[bb, aa, zs[k]], s_send.at[n], s_recv.at[n], seq, mate
        )

    lane = lax.broadcasted_iota(jnp.int32, (1, 4 * HALF), 1)
    zblock = (
        jnp.where(lane >= HALF, 1, 0)
        + jnp.where(lane >= 2 * HALF, 1, 0)
        + jnp.where(lane >= 3 * HALF, 1, 0)
    )
    within = lane - HALF * zblock
    qrow = lax.broadcasted_iota(jnp.int32, (q_ref.shape[0], 1), 0)
    qpos = qrow - jnp.where(qrow >= span_rows, span_rows, 0) + seq * span_rows

    def attend(buf, b, a, stride_a, stride_b, half):
        keys = buf[b, a].reshape(4 * HALF, KEYW)
        row = within + half * HALF
        owner = a * stride_a + b * stride_b + zblock * 4
        kpos = jnp.where(row < prior_rows, -1, owner * span_rows + row - prior_rows)
        s = lax.dot_general(
            q_ref[...], keys, (((1,), (1,)), ((), ())), preferred_element_type=jnp.float32
        )
        s = jnp.where(kpos <= qpos, s * scale, -1e30)
        m_old = mx[:, :1]
        m_new = jnp.maximum(m_old, jnp.max(s, axis=1, keepdims=True))
        alpha = jnp.exp(m_old - m_new)
        p = jnp.exp(s - m_new)
        sm[...] = sm[...] * alpha + jnp.sum(p, axis=1, keepdims=True)
        mx[...] = jnp.broadcast_to(m_new, mx.shape)
        acc[...] = acc[...] * alpha + jnp.dot(
            p.astype(jnp.bfloat16), keys[:, :LATW], preferred_element_type=jnp.float32
        )

    def attend_ring(h, j):
        attend(ring, m4(b0 + place(h)), m4(a0 + place(j)), sa, sb, core)

    def attend_sib(h, j):
        attend(sib, m4(a0 + place(h)), m4(b0 + place(j)), sb, sa, 1 - core)

    for k in range(3):
        z_copy(k).start()
    for i in range(2):
        a_copy(i, 0).start()
        b_copy(i, 0, 0).start()
    for k in (1, 2, 3):
        z_arrival(k - 1).wait_recv()
        for i in range(2):
            a_copy(i, k).start()
        for i in range(2):
            b_copy(i, 0, k).start()
        s_copy(0, 0, k).start()
    for k in range(4):
        for i in range(2):
            a_arrival(i, k).wait_recv()
            if k % 2 == i:
                a2_copy(k).start()
            j = (2, 1)[i]
            b_copy(0, j, k).start()
            b_copy(1, j, k).start()
            s_copy(0, j, k).start()
    attend_ring(0, 0)
    for k in range(4):
        a2_arrival(k).wait_recv()
        b_copy(0, 3, k).start()
        b_copy(1, 3, k).start()
        s_copy(0, 3, k).start()
    for k in (1, 2, 3):
        s_arrival(0, 0, k).wait_recv()
    attend_sib(0, 0)

    def first_b(j, carry):
        for k in range(4):
            for i in range(2):
                b_arrival(i, j, k).wait_recv()
                if k % 2 == i:
                    b2_copy(j, k).start()
                s_copy((2, 1)[i], j, k).start()
        attend_ring(1, j)
        attend_ring(2, j)
        return carry

    def column(j, carry):
        for k in range(4):
            s_arrival(0, j, k).wait_recv()
        attend_ring(0, j)
        attend_sib(0, j)
        return carry

    def first_b_sib(j, carry):
        for h in (1, 2):
            for k in range(4):
                s_arrival(h, j, k).wait_recv()
            attend_sib(h, j)
        return carry

    def last_b(j, carry):
        for k in range(4):
            b2_arrival(j, k).wait_recv()
            s_copy(3, j, k).start()
        attend_ring(3, j)
        return carry

    def last_sib(j, carry):
        for k in range(4):
            s_arrival(3, j, k).wait_recv()
        attend_sib(3, j)
        return carry

    def middle(j, carry):
        column(j, carry)
        first_b(j, carry)
        return carry

    first_b(0, 0)
    lax.fori_loop(1, 4, middle, 0)

    def closing(j, carry):
        first_b_sib(j, carry)
        last_b(j, carry)
        return carry

    lax.fori_loop(0, 4, closing, 0)
    lax.fori_loop(0, 4, last_sib, 0)
    out_ref[...] = (acc[...] / sm[:, :1]).astype(out_ref.dtype)

    for k in range(3):
        z_copy(k).wait_send()
    for k in range(4):
        for i in range(2):
            a_copy(i, k).wait_send()
        a2_copy(k).wait_send()

    def drain(j, carry):
        for k in range(4):
            for i in range(2):
                b_copy(i, j, k).wait_send()
            b2_copy(j, k).wait_send()
            for h in (1, 2, 3):
                s_copy(h, j, k).wait_send()
        return carry

    lax.fori_loop(0, 4, drain, 0)
    for k in (1, 2, 3):
        s_copy(0, 0, k).wait_send()

    def drain_column(j, carry):
        for k in range(4):
            s_copy(0, j, k).wait_send()
        return carry

    lax.fori_loop(1, 4, drain_column, 0)


def gathered_attention(queries, own_keys, scale, prior_rows, span_rows):
    rows = queries.shape[0]
    dma = pltpu.SemaphoreType.DMA
    return pl.pallas_call(
        functools.partial(attend_kernel, scale, prior_rows, span_rows),
        out_shape=jax.ShapeDtypeStruct((rows, LATW), jnp.bfloat16),
        in_specs=[pl.BlockSpec(memory_space=pltpu.VMEM)] * 2,
        out_specs=pl.BlockSpec(memory_space=pltpu.VMEM),
        scratch_shapes=[
            pltpu.VMEM((4, 4, 4, HALF, KEYW), jnp.bfloat16),
            pltpu.VMEM((4, 4, 4, HALF, KEYW), jnp.bfloat16),
            pltpu.VMEM((rows, LATW), jnp.float32),
            pltpu.VMEM((rows, 128), jnp.float32),
            pltpu.VMEM((rows, 128), jnp.float32),
            dma((2,)),
            dma((3,)),
            dma((3,)),
            dma((2, 4)),
            dma((2, 4)),
            dma((4,)),
            dma((4,)),
            dma((2, 16)),
            dma((2, 16)),
            dma((16,)),
            dma((16,)),
            dma((64,)),
            dma((64,)),
        ],
        name="gather_attend",
        compiler_params=pltpu.CompilerParams(
            collective_id=0, has_side_effects=True, vmem_limit_bytes=40 << 20
        ),
    )(queries, own_keys)


SLOTS = 4
BLOCK = 32


def expert_kernel(
    rows_ref,
    hidden_ref,
    wg_hbm,
    wu_hbm,
    wd_hbm,
    out_ref,
    toks,
    wg,
    wu,
    wd,
    outb,
    xin,
    kept,
    ysend,
    yrecv,
    back,
    got,
    part,
    fsend,
    frecv,
    bsend,
    brecv,
    w_sem,
    l_sem,
    agf_send,
    agf_recv,
    agb_send,
    agb_recv,
    d_send,
    d_recv,
    s_send,
    s_recv,
    y_send,
    y_recv,
    r_send,
    r_recv,
    f_send,
    f_recv,
    b_send,
    b_recv,
):
    seq = lax.axis_index("seq")
    rep = lax.axis_index("rep")
    core = lax.rem(rep, 2)
    zc = lax.rem(seq // 4, 4) * 2 + rep // 2
    zhi = lax.rem(seq // 4, 4)
    x0 = seq // 16
    y0 = lax.rem(seq, 4)
    here = x0 * 4 + y0
    way = 1 - 2 * core
    mate = rep + 1 - 2 * core
    width = hidden_ref.shape[1]

    def chip(z):
        z = lax.rem(z + 8, 8)
        return x0 * 16 + (z // 2) * 4 + y0, lax.rem(z, 2) * 2 + core

    ahead = chip(zc + way)
    behind = chip(zc - way)

    def to_peer(p):
        return lax.rem(x0 + p // 4, 4), lax.rem(y0 + lax.rem(p, 4), 4)

    def from_peer(p):
        return lax.rem(x0 + 4 - p // 4, 4), lax.rem(y0 + 4 - lax.rem(p, 4), 4)

    def plane_seq(xy):
        return xy[0] * 16 + zhi * 4 + xy[1]

    partners = [ahead, behind, (seq, mate)] + [(plane_seq(to_peer(p)), rep) for p in range(1, 16)]

    w_copies = [
        pltpu.make_async_copy(wg_hbm.at[0], wg, w_sem.at[0]),
        pltpu.make_async_copy(wu_hbm.at[0], wu, w_sem.at[1]),
        pltpu.make_async_copy(wd_hbm.at[0], wd, w_sem.at[2]),
    ]
    for copy in w_copies:
        copy.start()
    first = pltpu.make_async_copy(rows_ref, toks.at[0], l_sem.at[0])
    first.start()
    first.wait()
    greet(partners)

    def agf(k):
        source = (0, 1, 3, 5)[k]
        return remote(
            toks.at[source], toks.at[2 * k + 1], agf_send.at[k], agf_recv.at[k], ahead[0], ahead[1]
        )

    def agb(k):
        source = (0, 2, 4)[k]
        return remote(
            toks.at[source], toks.at[2 * k + 2], agb_send.at[k], agb_recv.at[k], behind[0], behind[1]
        )

    lane = lax.broadcasted_iota(jnp.int32, (1, 256), 1)
    code = (
        (((lane >> 6) * 16) + zhi * 4 + ((lane >> 4) & 3)) * SLOTS + (lane & 3)
    ).astype(jnp.float32)
    lane_block = (lane >> 2) & 3
    token_block = lax.broadcasted_iota(jnp.int32, (128, 1), 0) >> 5
    same_block = token_block == lane_block

    def tokens_of(ph):
        return toks[4 * ph : 4 * ph + 4].reshape(128, width + 128)

    def dispatch_copy(ph, p):
        xy = to_peer(p)
        return remote(
            outb.at[ph, xy[0] * 4 + xy[1]],
            xin.at[core, ph, here],
            d_send.at[ph, p],
            d_recv.at[ph, p],
            plane_seq(xy),
            rep,
        )

    def own_rows(ph):
        return pltpu.make_async_copy(
            outb.at[ph, here], xin.at[core, ph, here], l_sem.at[1 + ph]
        )

    def share(ph, p):
        xy = from_peer(p)
        slot = xin.at[core, ph, xy[0] * 4 + xy[1]]
        return remote(slot, slot, s_send.at[ph, p], s_recv.at[ph, p], seq, mate)

    def share_arrival(ph, p):
        xy = from_peer(p)
        slot = xin.at[1 - core, ph, xy[0] * 4 + xy[1]]
        return remote(slot, slot, s_send.at[ph, p], s_recv.at[ph, p], seq, mate)

    def dispatch(ph):
        block = tokens_of(ph)
        meta = block[:, width:].astype(jnp.float32)
        hit = meta[:, 0:1] == code
        for k in range(1, 6):
            hit = hit | (meta[:, k : k + 1] == code)
        pick = jnp.where(hit & same_block, 1.0, 0.0).astype(jnp.bfloat16)
        rows = lax.dot_general(
            pick, block[:, :width], (((0,), (0,)), ((), ())), preferred_element_type=jnp.float32
        )
        outb[ph] = rows.astype(jnp.bfloat16).reshape(16, 16, width)

        def send(p, carry):
            dispatch_copy(ph, p).start()
            return carry

        lax.fori_loop(1, 16, send, 0)
        own_rows(ph).start()

    def arrivals(ph):
        own_rows(ph).wait()
        share(ph, 0).start()

        def one(p, carry):
            dispatch_copy(ph, p).wait_recv()
            share(ph, p).start()
            return carry

        lax.fori_loop(1, 16, one, 0)

    def share_arrivals(ph):
        def one(p, carry):
            share_arrival(ph, p).wait_recv()
            return carry

        lax.fori_loop(0, 16, one, 0)

    def expert(which, ph):
        rows = xin[which, ph].reshape(256, width)
        across = (((1,), (1,)), ((), ()))
        gate = lax.dot_general(rows, wg[...], across, preferred_element_type=jnp.float32)
        up = lax.dot_general(rows, wu[...], across, preferred_element_type=jnp.float32)
        act = (jax.nn.silu(gate) * up).astype(jnp.bfloat16)
        return jnp.dot(act, wd[...], preferred_element_type=jnp.float32)

    def pair_copy(ph):
        return remote(ysend.at[ph], yrecv.at[ph], y_send.at[ph], y_recv.at[ph], seq, mate)

    def return_copy(ph, p):
        xy = to_peer(p)
        return remote(
            back.at[ph, xy[0] * 4 + xy[1]],
            got.at[ph, here],
            r_send.at[ph, p],
            r_recv.at[ph, p],
            plane_seq(xy),
            rep,
        )

    def own_back(ph):
        return pltpu.make_async_copy(back.at[ph, here], got.at[ph, here], l_sem.at[3 + ph])

    def give_back(ph):
        pair_copy(ph).wait_recv()
        total = kept[ph] + yrecv[ph].astype(jnp.float32)
        back[ph] = total.astype(jnp.bfloat16).reshape(16, 16, width)

        def send(p, carry):
            return_copy(ph, p).start()
            return carry

        lax.fori_loop(1, 16, send, 0)
        own_back(ph).start()

    def combine(ph):
        def one(p, carry):
            return_copy(ph, p).wait_recv()
            return carry

        lax.fori_loop(1, 16, one, 0)
        own_back(ph).wait()
        meta = toks[4 * ph : 4 * ph + 4, :, width:].reshape(128, 128).astype(jnp.float32)
        high = jnp.zeros((128, 256), jnp.float32)
        low = jnp.zeros((128, 256), jnp.float32)
        for k in range(6):
            hit = (meta[:, k : k + 1] == code) & same_block
            high = high + jnp.where(hit, meta[:, 6 + k : 7 + k], 0.0)
            low = low + jnp.where(hit, meta[:, 12 + k : 13 + k], 0.0)
        both = jnp.concatenate([high, low], axis=0).astype(jnp.bfloat16)
        sums = jnp.dot(both, got[ph].reshape(256, width), preferred_element_type=jnp.float32)
        part[4 * ph : 4 * ph + 4] = (sums[:128] + sums[128:]).reshape(4, BLOCK, width)

    agf(0).start()
    agb(0).start()
    agf(0).wait_recv()
    agf(1).start()
    agb(0).wait_recv()
    agb(1).start()
    agf(1).wait_recv()
    agf(2).start()
    dispatch(0)
    agb(1).wait_recv()
    agb(2).start()
    agf(2).wait_recv()
    agf(3).start()
    agb(2).wait_recv()
    agf(3).wait_recv()
    dispatch(1)
    for copy in w_copies:
        copy.wait()
    arrivals(0)
    kept[0] = expert(core, 0)
    share_arrivals(0)
    ysend[0] = expert(1 - core, 0).astype(jnp.bfloat16)
    pair_copy(0).start()
    arrivals(1)
    kept[1] = expert(core, 1)
    give_back(0)
    share_arrivals(1)
    ysend[1] = expert(1 - core, 1).astype(jnp.bfloat16)
    pair_copy(1).start()
    give_back(1)
    combine(0)
    combine(1)

    def f_copy(k):
        return remote(fsend.at[k], frecv.at[k], f_send.at[k], f_recv.at[k], ahead[0], ahead[1])

    def b_copy(k):
        return remote(bsend.at[k], brecv.at[k], b_send.at[k], b_recv.at[k], behind[0], behind[1])

    fsend[0] = part[7].astype(jnp.bfloat16)
    f_copy(0).start()
    bsend[0] = part[5].astype(jnp.bfloat16)
    b_copy(0).start()
    for k in range(1, 4):
        f_copy(k - 1).wait_recv()
        fsend[k] = (part[(7, 6, 4, 2)[k]] + frecv[k - 1].astype(jnp.float32)).astype(jnp.bfloat16)
        f_copy(k).start()
        if k < 3:
            b_copy(k - 1).wait_recv()
            bsend[k] = (part[(5, 3, 1)[k]] + brecv[k - 1].astype(jnp.float32)).astype(jnp.bfloat16)
            b_copy(k).start()
    b_copy(2).wait_recv()
    total = hidden_ref[...] + part[0] + brecv[2].astype(jnp.float32)
    f_copy(3).wait_recv()
    out_ref[...] = (total + frecv[3].astype(jnp.float32)).astype(out_ref.dtype)

    for k in range(4):
        agf(k).wait_send()
        f_copy(k).wait_send()
    for k in range(3):
        agb(k).wait_send()
        b_copy(k).wait_send()
    for ph in range(2):
        pair_copy(ph).wait_send()
        share(ph, 0).wait_send()

        def drain(p, carry):
            dispatch_copy(ph, p).wait_send()
            share(ph, p).wait_send()
            return_copy(ph, p).wait_send()
            return carry

        lax.fori_loop(1, 16, drain, 0)


def expert_layer(rows, hidden, w_gate, w_up, w_down):
    width = hidden.shape[1]
    hidden_units = w_gate.shape[1]
    dma = pltpu.SemaphoreType.DMA
    bf16 = jnp.bfloat16
    vmem = pl.BlockSpec(memory_space=pltpu.VMEM)
    anywhere = pl.BlockSpec(memory_space=pl.ANY)
    return pl.pallas_call(
        expert_kernel,
        out_shape=jax.ShapeDtypeStruct(hidden.shape, bf16),
        in_specs=[vmem, vmem, anywhere, anywhere, anywhere],
        out_specs=vmem,
        scratch_shapes=[
            pltpu.VMEM((8, BLOCK, width + 128), bf16),
            pltpu.VMEM((hidden_units, width), bf16),
            pltpu.VMEM((hidden_units, width), bf16),
            pltpu.VMEM((hidden_units, width), bf16),
            pltpu.VMEM((2, 16, 16, width), bf16),
            pltpu.VMEM((2, 2, 16, 16, width), bf16),
            pltpu.VMEM((2, 256, width), jnp.float32),
            pltpu.VMEM((2, 256, width), bf16),
            pltpu.VMEM((2, 256, width), bf16),
            pltpu.VMEM((2, 16, 16, width), bf16),
            pltpu.VMEM((2, 16, 16, width), bf16),
            pltpu.VMEM((8, BLOCK, width), jnp.float32),
            pltpu.VMEM((4, BLOCK, width), bf16),
            pltpu.VMEM((4, BLOCK, width), bf16),
            pltpu.VMEM((3, BLOCK, width), bf16),
            pltpu.VMEM((3, BLOCK, width), bf16),
            dma((3,)),
            dma((5,)),
            dma((4,)),
            dma((4,)),
            dma((3,)),
            dma((3,)),
            dma((2, 16)),
            dma((2, 16)),
            dma((2, 16)),
            dma((2, 16)),
            dma((2,)),
            dma((2,)),
            dma((2, 16)),
            dma((2, 16)),
            dma((4,)),
            dma((4,)),
            dma((3,)),
            dma((3,)),
        ],
        name="experts",
        compiler_params=pltpu.CompilerParams(
            collective_id=1, has_side_effects=True, vmem_limit_bytes=56 << 20
        ),
    )(rows, hidden, w_gate, w_up, w_down)


def on_device(
    tokens,
    prior_cache,
    attn_gain,
    q_weight,
    kv_weight,
    kv_gain,
    key_up,
    value_up,
    out_weight,
    moe_gain,
    router,
    expert_ids,
    w_gate,
    w_up,
    w_down,
    handover,
    lengths,
    request_owner,
    page_table,
):
    seq_count = lax.axis_size("seq")
    rep_count = lax.axis_size("rep")
    seq_index = lax.axis_index("seq")
    rep_index = lax.axis_index("rep")
    tok_dev = tokens.shape[0]
    quarter = tok_dev // rep_count
    prior_dev = prior_cache.shape[0]
    local_heads = key_up.shape[0]
    nope_width = key_up.shape[1]
    latent_width = key_up.shape[2]
    rope_width = q_weight.shape[1] // local_heads - nope_width
    prior_total = prior_dev * seq_count
    token_float = tokens.astype(jnp.float32)
    normed = rms_scale(token_float, attn_gain).astype(jnp.bfloat16)
    span_pos = seq_index * tok_dev + jnp.arange(tok_dev)
    positions = prior_total + span_pos
    projected = jnp.dot(normed, q_weight, preferred_element_type=jnp.float32).reshape(
        tok_dev, local_heads, nope_width + rope_width
    )
    q_nope = projected[..., :nope_width].astype(jnp.bfloat16)
    q_rope = rotate(projected[..., nope_width:], positions)
    q_latent = jnp.einsum("thn,hnc->htc", q_nope, key_up, preferred_element_type=jnp.float32)
    queries = (
        jnp.concatenate([q_latent, jnp.transpose(q_rope, (1, 0, 2))], axis=2)
        .astype(jnp.bfloat16)
        .reshape(local_heads * tok_dev, latent_width + rope_width)
    )
    score_scale = (nope_width + rope_width) ** (-0.5)
    block_keys = jnp.concatenate(
        [prior_cache, latent_keys(normed, positions, kv_weight, kv_gain, latent_width)], axis=0
    )
    spare = KEYW - latent_width - rope_width
    head_latent = gathered_attention(
        jnp.pad(queries, ((0, 0), (0, spare))),
        jnp.pad(block_keys, ((0, 0), (0, spare))),
        score_scale,
        prior_dev,
        tok_dev,
    ).reshape(local_heads, tok_dev, latent_width)
    heads_out = (
        jnp.einsum("htc,hcv->thv", head_latent, value_up, preferred_element_type=jnp.float32)
        .astype(jnp.bfloat16)
        .reshape(tok_dev, -1)
    )
    head_partial = jnp.dot(heads_out, out_weight, preferred_element_type=jnp.float32)
    top_count = expert_ids.shape[1]
    own_ids = lax.dynamic_slice_in_dim(expert_ids, rep_index * quarter, quarter, 0)
    flat_ids = own_ids.reshape(-1)
    flat_index = jnp.arange(flat_ids.shape[0])
    rank = jnp.sum(
        (
            (flat_ids[:, None] == flat_ids[None, :]) & (flat_index[None, :] < flat_index[:, None])
        ).astype(jnp.int32),
        axis=1,
    )
    target = (flat_ids * SLOTS + rank).reshape(quarter, top_count)
    attention = sent_and_summed(head_partial.astype(jnp.bfloat16), "rep", 0)
    own_tokens = lax.dynamic_slice_in_dim(tokens, rep_index * quarter, quarter, 0)
    hidden_own = own_tokens.astype(jnp.float32) + attention
    moe_own = rms_scale(hidden_own, moe_gain).astype(jnp.bfloat16)
    logits = jnp.dot(moe_own, router, preferred_element_type=jnp.float32)
    named = own_ids[:, :, None] == jnp.arange(router.shape[1])[None, None, :]
    chosen = jnp.sum(jnp.where(named, logits[:, None, :], 0.0), axis=2)
    gate_score = jax.nn.sigmoid(chosen)
    weights = route_scale * gate_score / jnp.sum(gate_score, axis=1, keepdims=True)
    high = lax.reduce_precision(weights, 8, 7)
    sent_rows = jnp.concatenate(
        [
            moe_own,
            target.astype(jnp.bfloat16),
            high.astype(jnp.bfloat16),
            (weights - high).astype(jnp.bfloat16),
            jnp.zeros((quarter, 128 - 3 * top_count), jnp.bfloat16),
        ],
        axis=1,
    )
    layer_out = expert_layer(
        sent_rows, hidden_own, jnp.swapaxes(w_gate, 1, 2), jnp.swapaxes(w_up, 1, 2), w_down
    )
    group_size = handover.shape[0]
    req_dev = group_size // seq_count
    owner_here = lax.dynamic_slice_in_dim(request_owner, rep_index * group_size, group_size, 0)
    request_index = jnp.arange(group_size)
    earlier = jnp.sum(
        (
            (owner_here[None, :] == owner_here[:, None])
            & (request_index[None, :] < request_index[:, None])
        ).astype(jnp.int32),
        axis=1,
    )
    order_key = owner_here * req_dev + earlier
    picked = jnp.argmax((order_key[None, :] == request_index[:, None]).astype(jnp.int32), axis=1)
    parcel = handover.at[picked].get(mode="promise_in_bounds")
    parcels = lax.all_to_all(parcel, "seq", split_axis=0, concat_axis=0, tiled=True)
    layers_here = handover.shape[1]
    pos_dev = handover.shape[2]
    row_width = handover.shape[3]
    maxlen = seq_count * pos_dev
    pages_per = maxlen // PAGE
    stacked = (
        parcels.reshape(seq_count, req_dev, layers_here, pos_dev, row_width)
        .transpose(1, 2, 0, 3, 4)
        .reshape(req_dev, layers_here, maxlen, row_width)
    )
    own_requests = (
        lax.dynamic_slice_in_dim(picked, seq_index * req_dev, req_dev, 0) + rep_index * group_size
    )
    own_lengths = lengths.at[own_requests].get(mode="promise_in_bounds")
    page_rows = (
        stacked.reshape(req_dev, layers_here, pages_per, PAGE, row_width)
        .transpose(0, 2, 1, 3, 4)
        .reshape(req_dev * pages_per, layers_here, PAGE, row_width)
    )
    physical = page_table.at[own_requests].get(mode="promise_in_bounds").reshape(-1)
    inverse = jnp.argmax(
        (physical[None, :] == jnp.arange(req_dev * pages_per)[:, None]).astype(jnp.int32), axis=1
    )
    page_start = lax.rem(inverse, pages_per) * PAGE
    page_length = own_lengths.at[inverse // pages_per].get(mode="promise_in_bounds")
    alive = page_start[:, None] + jnp.arange(PAGE)[None, :] < page_length[:, None]
    decode_pages = jnp.where(
        alive[:, None, :, None],
        page_rows.at[inverse].get(mode="promise_in_bounds"),
        jnp.zeros((), jnp.bfloat16),
    )
    return (layer_out, decode_pages)


def solution(mesh):
    return jax.shard_map(
        on_device,
        mesh=mesh,
        in_specs=(
            P("seq", None),
            P("seq", None),
            P(),
            P(None, "rep"),
            P(),
            P(),
            P("rep", None, None),
            P("rep", None, None),
            P("rep", None),
            P(),
            P(),
            P("seq", None),
            P("seq", None, "rep"),
            P("seq", None, "rep"),
            P("seq", "rep", None),
            P("rep", None, "seq", None),
            P(),
            P(),
            P(),
        ),
        out_specs=(P(("seq", "rep"), None), P(("seq", "rep"), None, None, None)),
        check_vma=False,
    )
```
